128 devices in a mesh: wide: 32 (over y, z_lo, x), narrow: 4 (over z_hi, core).
Axes of the slice: x: 4, y: 4, z: 4 (z_hi: 2, z_lo: 2; z = z_hi * 2 + z_lo), core: 2. Of those that a mesh axis runs over, the one named last changes fastest.
Arguments:
- loads: float32 [98304, 512], P('wide', 'narrow'), may hold values from -6 to 6
- start: float32 [98304, 512], P('wide', 'narrow'), may hold values from -6 to 6
- stiffness: bfloat16 [128, 1024, 1024], P('wide')
- local_inverse: bfloat16 [128, 1024, 1024], P('wide')
- modes: bfloat16 [128, 1024, 32], P('wide'), may hold values from -0.1875 to 0.1875
- coarse_inverse: float32 [4096, 4096], P('wide', 'narrow'), as said below
- margin_rows: int32 [128, 256], P('wide'), may hold values from 0 to 98303, as said below
Outputs:
- displacement: float32 [98304, 512], P('wide', 'narrow')
- final_residual: float32 [98304, 512], P('wide', 'narrow')
The draws below stay inside these ranges and needn't reach their ends.
Inputs may be any that keep to these rules, and one draw needn't show every extreme that they name: Row s lists 256 distinct rows of loads, none of them rows s * 768 to s * 768 + 767. Call rows i * 4 * 768 to (i + 1) * 4 * 768 - 1 block i. For every i, the entries of rows i * 4 to (i + 1) * 4 - 1 of margin_rows fall at most 48 times into any one block, and exactly 48 times into some block. coarse_inverse equals its transpose.
All inputs are finite; a program needn't handle non-finite values.
Results may differ from the reference program's by a relative error of at most 0.0062.
Values may be sent and summed in bfloat16 or wider, within the bound.
A program may use at most 128 MiB of HBM per device.

```python
import math
import jax
import jax.numpy as jnp
from jax import lax

SUBN = 1024
OVL = 256
MODES = 32
SUB_DEV = 4
COLS = 512
ITERS = 2
CORE = 768
NSUB = 128
NC = 4096
NDOF = 98304


def with_diagonal(random_part, key_diag, lowest, highest):
    lead_shape = random_part.shape[:-1]
    matrix_order = random_part.shape[-1]
    log_diag = jax.random.uniform(key_diag, lead_shape, jnp.float32, math.log(lowest), math.log(highest))
    identity = jnp.eye(matrix_order, dtype=jnp.float32)
    return random_part * (1.0 - identity) + identity * jnp.exp(log_diag)[..., None]


def draw_stiffness(key, part):
    key_off, key_diag = jax.random.split(jax.random.fold_in(key, 11))
    random_part = jax.random.normal(key_off, (NSUB, SUBN, SUBN), jnp.float32)
    return with_diagonal(random_part * (0.6 / math.sqrt(SUBN)), key_diag, 1.0, 2.0).astype(jnp.bfloat16)


def draw_local_inverse(key, part):
    key_off, key_diag = jax.random.split(jax.random.fold_in(key, 23))
    random_part = jax.random.normal(key_off, (NSUB, SUBN, SUBN), jnp.float32)
    return with_diagonal(random_part * (0.3 / math.sqrt(SUBN)), key_diag, 0.5, 1.0).astype(jnp.bfloat16)


def draw_coarse_inverse(key, part):
    key_off, key_diag = jax.random.split(jax.random.fold_in(key, 37))
    random_part = jax.random.normal(key_off, (NC, NC), jnp.float32)
    symmetric = (random_part + random_part.T) * 0.70710678
    return with_diagonal(symmetric * (2.0 / math.sqrt(NC)), key_diag, 0.5, 1.0)


def pick_from(table, block_of):
    return jnp.take_along_axis(table, block_of, axis=1)


def draw_margin_rows(key, part):
    owners = NSUB // SUB_DEV
    average = SUB_DEV * OVL // owners
    spread_most = average // 2
    halves = owners // 2
    core_count = SUBN - OVL
    key_lift, key_pick, key_sign, key_slot, key_self, key_start = jax.random.split(jax.random.fold_in(key, 51), 6)
    deviation = jax.random.randint(key_lift, (owners, halves), 0, spread_most + 1)
    chosen = jax.random.randint(key_pick, (owners, 1), 0, halves)
    deviation = jnp.where(jnp.arange(halves, dtype=jnp.int32)[None, :] == chosen, spread_most, deviation)
    direction = jax.random.randint(key_sign, (owners, halves), 0, 2) * 2 - 1
    counts = jnp.stack([average + direction * deviation, average - direction * deviation], axis=2).reshape(owners, owners)
    block_end = jnp.cumsum(counts, axis=1)
    starts = block_end - counts
    source_slot = jax.random.randint(key_slot, (owners, owners), 0, SUB_DEV)
    self_slot = jax.random.randint(key_self, (owners, 1), 1, SUB_DEV)
    source_slot = jnp.where(jnp.arange(owners, dtype=jnp.int32)[None, :] == 0, self_slot, source_slot)
    window = jax.random.randint(key_start, (owners, owners), 0, core_count - counts + 1)
    positions = jnp.arange(SUB_DEV * OVL, dtype=jnp.int32)
    block_of = jnp.sum((block_end[:, None, :] <= positions[None, :, None]).astype(jnp.int32), axis=2)
    source = (jnp.arange(owners, dtype=jnp.int32)[:, None] + block_of) % owners
    global_rows = source * (SUB_DEV * core_count) + pick_from(source_slot, block_of) * core_count
    global_rows = global_rows + pick_from(window, block_of) + positions[None, :] - pick_from(starts, block_of)
    return global_rows.reshape(NSUB, OVL).astype(jnp.int32)


def level_of(stream_key, dims, cuts, least, top_value):
    loudness, own = 1.0, jax.random.fold_in(stream_key, 6)
    for axis_at, blocks in cuts:
        steps = jnp.exp(jax.random.uniform(jax.random.fold_in(own, axis_at), (blocks,), jnp.float32, least / len(cuts), top_value / len(cuts)))
        loudness = loudness * jnp.repeat(steps, dims[axis_at] // blocks).reshape([-1 if axis == axis_at else 1 for axis in range(len(dims))])
    return loudness


def scatter_about(key, shape, scale, most, pieces=(), kind=jnp.bfloat16):
    values = jax.random.normal(key, shape, jnp.float32) * scale
    if len(pieces) > 0:
        values = level_of(key, shape, pieces, -0.22, 0.18) * values
    return jnp.clip(values, min=-most, max=most).astype(kind)


def setup_inputs(seed: int = 0) -> dict:
    arg_keys = jax.random.split(jax.random.key(seed), 8)
    return {
        "loads": scatter_about(arg_keys[0], (NDOF, COLS), 1.0, 6.0, ((0, 32), (1, 4)), jnp.float32),
        "start": scatter_about(arg_keys[1], (NDOF, COLS), 1.0, 6.0, ((0, 32), (1, 4)), jnp.float32),
        "stiffness": draw_stiffness(jax.random.fold_in(arg_keys[7], 71), 0),
        "local_inverse": draw_local_inverse(jax.random.fold_in(arg_keys[7], 71), 0),
        "modes": scatter_about(arg_keys[4], (NSUB, SUBN, MODES), SUBN ** -0.5, 0.1875, ((0, 32),)),
        "coarse_inverse": draw_coarse_inverse(jax.random.fold_in(arg_keys[7], 71), 0),
        "margin_rows": draw_margin_rows(jax.random.fold_in(arg_keys[7], 71), 0),
    }


damping = 0.5


def gather_local(field, margin_rows):
    core_part = field.reshape(NSUB, CORE, COLS)
    outer_part = field[margin_rows.reshape(-1)].reshape(NSUB, OVL, COLS)
    return jnp.concatenate([core_part, outer_part], axis=1).astype(jnp.bfloat16)


def assemble_parts(parts, margin_rows):
    summed = parts[:, :CORE, :].reshape(NSUB * CORE, COLS)
    return summed.at[margin_rows.reshape(-1)].add(parts[:, CORE:, :].reshape(NSUB * OVL, COLS))


def apply_each(matrices, vectors):
    def single(operands):
        return jnp.dot(operands[0].astype(jnp.float32), operands[1].astype(jnp.float32), precision=lax.Precision.HIGHEST)
    return lax.map(single, (matrices, vectors))


def project_modes(modes, vectors):
    def single(operands):
        return jnp.dot(operands[0].astype(jnp.float32).T, operands[1].astype(jnp.float32), precision=lax.Precision.HIGHEST)
    return lax.map(single, (modes, vectors))


def residual_of(field, loads, stiffness, margin_rows):
    return loads - assemble_parts(apply_each(stiffness, gather_local(field, margin_rows)), margin_rows)


def reference(loads, start, stiffness, local_inverse, modes, coarse_inverse, margin_rows):
    field = start
    for iteration in range(ITERS):
        residual = residual_of(field, loads, stiffness, margin_rows)
        restricted = gather_local(residual, margin_rows)
        solved_local = apply_each(local_inverse, restricted)
        projection = project_modes(modes, restricted).reshape(NC, COLS)
        coarse = jnp.dot(coarse_inverse, projection, precision=lax.Precision.HIGHEST).reshape(NSUB, MODES, COLS)
        lifted = apply_each(modes, coarse)
        field = field + assemble_parts(damping * solved_local + lifted, margin_rows)
    return field, residual_of(field, loads, stiffness, margin_rows)
```

```python
import jax
import jax.numpy as jnp
from jax import lax
from jax.experimental import pallas as pl
from jax.experimental.pallas import tpu as pltpu
from jax.sharding import PartitionSpec as P

MESH = pl.DeviceIdType.MESH
ITERS = 2
SUBS = 4
ORDER = 1024
CORE = 768
MARGIN = ORDER - CORE
COLS = 128
MODES = 32
HELD = SUBS * CORE
OUTER = SUBS * MARGIN
OWNERS = 32
ACROSS = 4
CAP = 48
SLOTS = OWNERS * CAP
COARSE = SUBS * MODES
WIDTH = 1024
STRIP = 128
F32 = jnp.float32
BF16 = jnp.bfloat16
GATHER, SCATTER, REGATHER, CORRECT = 0, 1, 2, 3


def dot(a, b):
    return jnp.dot(a, b, preferred_element_type=F32)


def iota(shape, axis):
    return lax.broadcasted_iota(jnp.int32, shape, axis).astype(F32)


def strip(i):
    return pl.ds(pl.multiple_of(i * STRIP, STRIP), STRIP)


def split_digits(v):
    high = jnp.floor(v * (1.0 / 64.0))
    return high.astype(BF16), (v - high * 64.0).astype(BF16)


def store_column(row, ref):
    same = iota((STRIP, STRIP), 0) == iota((STRIP, STRIP), 1)
    for k in range(row.shape[1] // STRIP):
        piece = jnp.broadcast_to(row[:, k * STRIP:(k + 1) * STRIP], (STRIP, STRIP))
        column = jnp.sum(jnp.where(same, piece, 0.0), axis=1, keepdims=True)
        ref[k * STRIP:(k + 1) * STRIP, :] = jnp.broadcast_to(column, (STRIP, STRIP))


def fill_by_column(out, column):
    rows, width = out.shape

    def body(i, _):
        held = column[strip(i), :]
        lanes = iota((STRIP, STRIP), 1)
        for k in range(width // STRIP):
            out[strip(i), k * STRIP:(k + 1) * STRIP] = jnp.where(held == lanes + float(k * STRIP), 1.0, 0.0).astype(BF16)
        return 0

    lax.fori_loop(0, rows // STRIP, body, 0)


def fill_by_row(out, row):
    rows, width = out.shape

    def body(i, _):
        down = (lax.broadcasted_iota(jnp.int32, (STRIP, STRIP), 0) + i * STRIP).astype(F32)
        for k in range(width // STRIP):
            out[strip(i), k * STRIP:(k + 1) * STRIP] = jnp.where(down == row[:, k * STRIP:(k + 1) * STRIP], 1.0, 0.0).astype(BF16)
        return 0

    lax.fori_loop(0, rows // STRIP, body, 0)


def fill_equal(out, column, row):
    rows, width = out.shape

    def body(i, _):
        held = column[strip(i), :]
        for k in range(width // STRIP):
            out[strip(i), k * STRIP:(k + 1) * STRIP] = jnp.where(held == row[:, k * STRIP:(k + 1) * STRIP], 1.0, 0.0).astype(BF16)
        return 0

    lax.fori_loop(0, rows // STRIP, body, 0)


def kernel(
    loads, start, stiffness, local_inverse, modes, coarse_inverse, margin_rows,
    out_x, out_r,
    k_v, l_v, m_v, mt_v, c_in, c_all, x, base, pair, loc, part, picked,
    pick, pick_t, same, take, take_t, placed_row, wanted_row,
    outer, asked, wanted, send, recv, proj, bring, recv_sem, send_sem, index_sem, proj_sem, coarse_sem,
):
    me = lax.axis_index("wide")
    col = lax.axis_index("narrow")
    barrier = pltpu.get_barrier_semaphore()

    def greet(d, _):
        pl.semaphore_signal(barrier, inc=1, device_id=(lax.rem(me + d, OWNERS), col), device_id_type=MESH)
        return 0

    lax.fori_loop(1, OWNERS, greet, 0)
    for d in range(1, ACROSS):
        pl.semaphore_signal(barrier, inc=1, device_id=(me, lax.rem(col + d, ACROSS)), device_id_type=MESH)

    fetch_start = pltpu.make_async_copy(start, x, bring.at[0])
    fetch_coarse = pltpu.make_async_copy(coarse_inverse, c_in, bring.at[1])
    fetch_stiff = pltpu.make_async_copy(stiffness, k_v, bring.at[2])
    fetch_modes = pltpu.make_async_copy(modes, m_v, bring.at[3])
    fetch_local = pltpu.make_async_copy(local_inverse, l_v, bring.at[4])
    fetch_start.start()
    fetch_coarse.start()
    fetch_stiff.start()
    fetch_modes.start()
    fetch_local.start()

    rows = jnp.concatenate([margin_rows[s:s + 1, :] for s in range(SUBS)], axis=1).astype(F32)
    source = jnp.floor((rows + 0.5) * (1.0 / HELD))
    within = rows - source * HELD
    owned = source == iota((OWNERS, OUTER), 0)
    owned_b = jnp.where(owned, 1.0, 0.0).astype(BF16)

    def earlier(i, _):
        down = (lax.broadcasted_iota(jnp.int32, (STRIP, OUTER), 0) + i * STRIP).astype(F32)
        take[strip(i), :OUTER] = jnp.where(down < iota((STRIP, OUTER), 1), 1.0, 0.0).astype(BF16)
        return 0

    lax.fori_loop(0, OUTER // STRIP, earlier, 0)
    before = dot(owned_b, take[:, :OUTER])
    rank = jnp.sum(jnp.where(owned, before, 0.0), axis=0, keepdims=True)
    placed = source * CAP + rank
    placed_row[...] = placed

    store_column(rank, picked.at[:OUTER])
    ranked = picked[:OUTER, :] == iota((OUTER, STRIP), 1)
    store_column(within + 1.0, picked.at[:OUTER])
    high, low = split_digits(jnp.where(ranked, picked[:OUTER, :], 0.0))
    ask = dot(owned_b, high) * 64.0 + dot(owned_b, low)
    asked[...] = jnp.broadcast_to(ask[:, None, :], (OWNERS, 8, STRIP))

    pl.semaphore_wait(barrier, OWNERS - 1 + ACROSS - 1)

    def ask_owner(d, _):
        peer = lax.rem(me + d, OWNERS)
        pltpu.make_async_remote_copy(
            asked.at[peer], wanted.at[me], index_sem.at[0], index_sem.at[1], device_id=(peer, col), device_id_type=MESH
        ).start()
        return 0

    lax.fori_loop(1, OWNERS, ask_owner, 0)
    wanted[pl.ds(me, 1)] = asked[pl.ds(me, 1)]

    store_column(placed, picked.at[:OUTER])
    fill_by_column(take, picked)
    fill_by_row(take_t, placed_row)

    fetch_coarse.wait()
    c_all[pl.ds(col, 1)] = c_in[...].astype(BF16)[None]
    for d in range(1, ACROSS):
        pltpu.make_async_remote_copy(
            c_all.at[col], c_all.at[col], coarse_sem.at[0], coarse_sem.at[1],
            device_id=(me, lax.rem(col + d, ACROSS)), device_id_type=MESH,
        ).start()

    for k in range(2):
        pltpu.make_async_copy(wanted.at[pl.ds(0, OWNERS - 1)], wanted.at[pl.ds(0, OWNERS - 1)], index_sem.at[k]).wait()
    slot_of = jnp.max(wanted[...], axis=1)
    high, low = split_digits(slot_of)
    slot = iota((STRIP, SLOTS), 1)
    owner_of = jnp.floor((slot + 0.5) * (1.0 / CAP))
    spread = jnp.where(slot - owner_of * CAP == iota((STRIP, SLOTS), 0), 1.0, 0.0).astype(BF16)
    wide = dot(high, spread) * 64.0 + dot(low, spread)
    row = jnp.sum(jnp.where(owner_of[:OWNERS] == iota((OWNERS, SLOTS), 0), wide, 0.0), axis=0, keepdims=True) - 1.0
    wanted_row[...] = row
    store_column(jnp.where(row < 0.0, -2.0, row), picked)
    fill_by_column(pick, picked)

    def ship(which):
        half = which % 2

        def one(d, _):
            peer = lax.rem(me + d, OWNERS)
            pltpu.make_async_remote_copy(
                send.at[half, peer], recv.at[which, me], send_sem.at[which], recv_sem.at[which],
                device_id=(peer, col), device_id_type=MESH,
            ).start()
            return 0

        lax.fori_loop(1, OWNERS, one, 0)
        recv[which, pl.ds(me, 1)] = send[half, pl.ds(me, 1)]

    def arrive(which):
        others = recv.at[which, pl.ds(0, OWNERS - 1)]
        pltpu.make_async_copy(others, others, recv_sem.at[which]).wait()
        pltpu.make_async_copy(others, others, send_sem.at[which]).wait()

    TILE = 384
    EACH = TILE // CAP

    def tile(i):
        return pl.ds(pl.multiple_of(i * TILE, TILE), TILE)

    def put(half, i, value):
        send[half, pl.ds(i * EACH, EACH)] = value.astype(BF16).reshape(EACH, CAP, COLS)

    def received(which):
        return recv[which].reshape(SLOTS, COLS)

    def spread_margin(half):
        def body(i, _):
            put(half, i, dot(take_t[tile(i), :], outer[...]))
            return 0

        lax.fori_loop(0, SLOTS // TILE, body, 0)

    def collect_margin(which):
        def body(s, _):
            block = take[pl.ds(pl.multiple_of(s * MARGIN, MARGIN), MARGIN), :]
            loc[s, CORE:, :] = dot(block, received(which)).astype(BF16)
            return 0

        lax.fori_loop(0, SUBS, body, 0)

    def rows_of(s):
        return pl.ds(pl.multiple_of(s * CORE, CORE), CORE)

    def margin_of(s):
        return pl.ds(pl.multiple_of(s * MARGIN, MARGIN), MARGIN)

    def pick_pairs():
        def split(s, _):
            v = base[rows_of(s), :]
            upper = v.astype(BF16)
            pair[rows_of(s), :COLS] = upper
            pair[rows_of(s), COLS:] = (v - upper.astype(F32)).astype(BF16)
            return 0

        lax.fori_loop(0, SUBS, split, 0)

        def body(i, _):
            both = dot(pick[tile(i), :], pair[...])
            picked[tile(i), :] = both[:, :COLS] + both[:, COLS:]
            return 0

        lax.fori_loop(0, SLOTS // TILE, body, 0)

    def correct_picked(half, which, sign):
        def body(i, _):
            put(half, i, picked[tile(i), :] + sign * dot(same[tile(i), :], received(which)))
            return 0

        lax.fori_loop(0, SLOTS // TILE, body, 0)

    fetch_start.wait()

    def lower(s, _):
        pair[rows_of(s), :COLS] = x[rows_of(s), :].astype(BF16)
        return 0

    lax.fori_loop(0, SUBS, lower, 0)

    def first(i, _):
        put(GATHER % 2, i, dot(pick[tile(i), :], pair[:, :COLS]))
        return 0

    lax.fori_loop(0, SLOTS // TILE, first, 0)
    ship(GATHER)

    fill_equal(same, picked, wanted_row)
    fill_by_row(pick_t, wanted_row)

    fetch_modes.wait()
    unit = jnp.where(iota((MODES, MODES), 0) == iota((MODES, MODES), 1), 1.0, 0.0).astype(BF16)
    for s in range(SUBS):
        mt_v[s] = lax.dot_general(unit, m_v[s], (((1,), (1,)), ((), ())), preferred_element_type=F32).astype(BF16)
    fetch_stiff.wait()

    def iteration(it, _):
        fetch_loads = pltpu.make_async_copy(loads, base, bring.at[5])
        fetch_loads.start()

        def from_core(s, _):
            loc[s, :CORE, :] = x[rows_of(s), :].astype(BF16)
            part[s] = dot(k_v[s, :, :CORE], loc[s, :CORE, :])
            return 0

        lax.fori_loop(0, SUBS, from_core, 0)
        arrive(GATHER)
        collect_margin(GATHER)

        def margin_part(s, _):
            outer[margin_of(s), :] = (part[s, CORE:, :] + dot(k_v[s, CORE:, CORE:], loc[s, CORE:, :])).astype(BF16)
            return 0

        lax.fori_loop(0, SUBS, margin_part, 0)
        spread_margin(SCATTER % 2)
        ship(SCATTER)
        fetch_loads.wait()

        def core_part(s, _):
            base[rows_of(s), :] = base[rows_of(s), :] - (part[s, :CORE, :] + dot(k_v[s, :CORE, CORE:], loc[s, CORE:, :]))
            return 0

        lax.fori_loop(0, SUBS, core_part, 0)

        @pl.when(it < ITERS)
        def _():
            pick_pairs()

        arrive(SCATTER)

        @pl.when(it < ITERS)
        def _():
            correct_picked(REGATHER % 2, SCATTER, -1.0)
            ship(REGATHER)

        def finish_residual(s, _):
            base[rows_of(s), :] = base[rows_of(s), :] - dot(pick_t[rows_of(s), :], received(SCATTER))
            return 0

        lax.fori_loop(0, SUBS, finish_residual, 0)

        @pl.when(it < ITERS)
        def _():
            @pl.when(it == 0)
            def _():
                fetch_local.wait()
                for k in range(2):
                    pltpu.make_async_copy(c_all.at[pl.ds(0, 3)], c_all.at[pl.ds(0, 3)], coarse_sem.at[k]).wait()

            def solve_core(s, _):
                loc[s, :CORE, :] = base[rows_of(s), :].astype(BF16)
                part[s] = dot(l_v[s, :, :CORE], loc[s, :CORE, :])
                return 0

            lax.fori_loop(0, SUBS, solve_core, 0)
            arrive(REGATHER)
            collect_margin(REGATHER)
            projected = [dot(mt_v[s], loc[s]) for s in range(SUBS)]
            proj[pl.ds(me, 1)] = jnp.concatenate(projected, axis=0).astype(BF16)[None]

            def share(d, _):
                pltpu.make_async_remote_copy(
                    proj.at[me], proj.at[me], proj_sem.at[0], proj_sem.at[1],
                    device_id=(lax.rem(me + d, OWNERS), col), device_id_type=MESH,
                ).start()
                return 0

            lax.fori_loop(1, OWNERS, share, 0)

            def solve_margin(s, _):
                whole = part[s] + dot(l_v[s, :, CORE:], loc[s, CORE:, :])
                base[rows_of(s), :] = x[rows_of(s), :] + 0.5 * whole[:CORE]
                part[s, CORE:, :] = 0.5 * whole[CORE:]
                return 0

            lax.fori_loop(0, SUBS, solve_margin, 0)
            for k in range(2):
                pltpu.make_async_copy(
                    proj.at[pl.ds(0, OWNERS - 1)], proj.at[pl.ds(0, OWNERS - 1)], proj_sem.at[k]
                ).wait()
            per = WIDTH // COARSE
            coarse = dot(c_all[0], proj[:per].reshape(WIDTH, COLS))
            for n in range(1, ACROSS):
                coarse = coarse + dot(c_all[n], proj[n * per:(n + 1) * per].reshape(WIDTH, COLS))
            coarse = coarse.astype(BF16)
            for s in range(SUBS):
                mine = coarse[s * MODES:(s + 1) * MODES]
                outer[s * MARGIN:(s + 1) * MARGIN, :] = (part[s, CORE:, :] + dot(m_v[s, CORE:, :], mine)).astype(BF16)
            spread_margin(CORRECT % 2)
            ship(CORRECT)
            for s in range(SUBS):
                mine = coarse[s * MODES:(s + 1) * MODES]
                base[s * CORE:(s + 1) * CORE, :] = base[s * CORE:(s + 1) * CORE, :] + dot(m_v[s, :CORE, :], mine)
            pick_pairs()
            arrive(CORRECT)
            correct_picked(GATHER % 2, CORRECT, 1.0)
            ship(GATHER)

            def finish_step(s, _):
                x[rows_of(s), :] = base[rows_of(s), :] + dot(pick_t[rows_of(s), :], received(CORRECT))
                return 0

            lax.fori_loop(0, SUBS, finish_step, 0)

        return 0

    lax.fori_loop(0, ITERS + 1, iteration, 0)
    give_x = pltpu.make_async_copy(x, out_x, bring.at[6])
    give_r = pltpu.make_async_copy(base, out_r, bring.at[7])
    give_x.start()
    give_r.start()
    give_x.wait()
    give_r.wait()


def shards(loads, start, stiffness, local_inverse, modes, coarse_inverse, margin_rows):
    field = jax.ShapeDtypeStruct((HELD, COLS), F32)
    hbm = pl.BlockSpec(memory_space=pl.ANY)
    return pl.pallas_call(
        kernel,
        out_shape=(field, field),
        in_specs=[hbm] * 6 + [pl.BlockSpec(memory_space=pltpu.VMEM)],
        out_specs=(hbm, hbm),
        scratch_shapes=[
            pltpu.VMEM((SUBS, ORDER, ORDER), BF16),
            pltpu.VMEM((SUBS, ORDER, ORDER), BF16),
            pltpu.VMEM((SUBS, ORDER, MODES), BF16),
            pltpu.VMEM((SUBS, MODES, ORDER), BF16),
            pltpu.VMEM((COARSE, WIDTH), F32),
            pltpu.VMEM((ACROSS, COARSE, WIDTH), BF16),
            pltpu.VMEM((HELD, COLS), F32),
            pltpu.VMEM((HELD, COLS), F32),
            pltpu.VMEM((HELD, 2 * COLS), BF16),
            pltpu.VMEM((SUBS, ORDER, COLS), BF16),
            pltpu.VMEM((SUBS, ORDER, COLS), F32),
            pltpu.VMEM((SLOTS, COLS), F32),
            pltpu.VMEM((SLOTS, HELD), BF16),
            pltpu.VMEM((HELD, SLOTS), BF16),
            pltpu.VMEM((SLOTS, SLOTS), BF16),
            pltpu.VMEM((OUTER, SLOTS), BF16),
            pltpu.VMEM((SLOTS, OUTER), BF16),
            pltpu.VMEM((1, OUTER), F32),
            pltpu.VMEM((1, SLOTS), F32),
            pltpu.VMEM((OUTER, COLS), BF16),
            pltpu.VMEM((OWNERS, 8, STRIP), F32),
            pltpu.VMEM((OWNERS, 8, STRIP), F32),
            pltpu.VMEM((2, OWNERS, CAP, COLS), BF16),
            pltpu.VMEM((4, OWNERS, CAP, COLS), BF16),
            pltpu.VMEM((OWNERS, COARSE, COLS), BF16),
            pltpu.SemaphoreType.DMA((8,)),
            pltpu.SemaphoreType.DMA((4,)),
            pltpu.SemaphoreType.DMA((4,)),
            pltpu.SemaphoreType.DMA((2,)),
            pltpu.SemaphoreType.DMA((2,)),
            pltpu.SemaphoreType.DMA((2,)),
        ],
        compiler_params=pltpu.CompilerParams(
            collective_id=0, has_side_effects=True, vmem_limit_bytes=63 * 1024 * 1024
        ),
    )(loads, start, stiffness, local_inverse, modes, coarse_inverse, margin_rows)


def solution(mesh):
    placed = (
        P("wide", "narrow"),
        P("wide", "narrow"),
        P("wide", None, None),
        P("wide", None, None),
        P("wide", None, None),
        P("wide", "narrow"),
        P("wide", None),
    )
    return jax.shard_map(
        shards,
        mesh=mesh,
        in_specs=placed,
        out_specs=(P("wide", "narrow"), P("wide", "narrow")),
        check_vma=False,
    )
```

```python
import jax
import jax.numpy as jnp
from jax import lax
from jax.experimental import pallas as pl
from jax.experimental.pallas import tpu as pltpu
from jax.sharding import PartitionSpec as P

MESH = pl.DeviceIdType.MESH
ITERS = 2
SUBS = 4
ORDER = 1024
TILE = 384
CORE = 768
MARGIN = ORDER - CORE
COLS = 128
MODES = 32
HELD = SUBS * CORE
OUTER = SUBS * MARGIN
OWNERS = 32
ACROSS = 4
CAP = 48
SLOTS = OWNERS * CAP
TILES = SLOTS // TILE
EACH = TILE // CAP
COARSE = SUBS * MODES
WIDTH = 1024
STRIP = 128
F32 = jnp.float32
BF16 = jnp.bfloat16
GATHER, SCATTER, REGATHER, CORRECT = 0, 1, 2, 3
SIDES = (4, 2, 4)


def reach(offset):
    return sum(min(o, n - o) for o, n in zip(offset, SIDES))


OFFSETS = sorted(
    [(dy, dz, dx) for dy in range(SIDES[0]) for dz in range(SIDES[1]) for dx in range(SIDES[2])],
    key=reach, reverse=True,
)
BACK = [OFFSETS.index(tuple((n - o) % n for o, n in zip(offset, SIDES))) for offset in OFFSETS]
SELF = OWNERS - 1


def dot(a, b):
    return jnp.dot(a, b, preferred_element_type=F32)


def iota(shape, axis):
    return lax.broadcasted_iota(jnp.int32, shape, axis).astype(F32)


def strip(i):
    return pl.ds(pl.multiple_of(i * STRIP, STRIP), STRIP)


def split_digits(v):
    high = jnp.floor(v * (1.0 / 64.0))
    return high.astype(BF16), (v - high * 64.0).astype(BF16)


def store_column(row, ref):
    same = iota((STRIP, STRIP), 0) == iota((STRIP, STRIP), 1)
    for k in range(row.shape[1] // STRIP):
        piece = jnp.broadcast_to(row[:, k * STRIP:(k + 1) * STRIP], (STRIP, STRIP))
        column = jnp.sum(jnp.where(same, piece, 0.0), axis=1, keepdims=True)
        ref[k * STRIP:(k + 1) * STRIP, :] = jnp.broadcast_to(column, (STRIP, STRIP))


def fill_by_column(out, column):
    rows, width = out.shape

    def body(i, _):
        held = column[strip(i), :]
        lanes = iota((STRIP, STRIP), 1)
        for k in range(width // STRIP):
            out[strip(i), k * STRIP:(k + 1) * STRIP] = jnp.where(held == lanes + float(k * STRIP), 1.0, 0.0).astype(BF16)
        return 0

    lax.fori_loop(0, rows // STRIP, body, 0)


def fill_by_row(out, row):
    rows, width = out.shape

    def body(i, _):
        down = (lax.broadcasted_iota(jnp.int32, (STRIP, STRIP), 0) + i * STRIP).astype(F32)
        for k in range(width // STRIP):
            out[strip(i), k * STRIP:(k + 1) * STRIP] = jnp.where(down == row[:, k * STRIP:(k + 1) * STRIP], 1.0, 0.0).astype(BF16)
        return 0

    lax.fori_loop(0, rows // STRIP, body, 0)


def fill_equal(out, column, row):
    rows, width = out.shape

    def body(i, _):
        held = column[strip(i), :]
        for k in range(width // STRIP):
            out[strip(i), k * STRIP:(k + 1) * STRIP] = jnp.where(held == row[:, k * STRIP:(k + 1) * STRIP], 1.0, 0.0).astype(BF16)
        return 0

    lax.fori_loop(0, rows // STRIP, body, 0)


def kernel(
    loads, start, stiffness, local_inverse, modes_t, coarse_inverse, margin_rows,
    out_x, out_r,
    k_v, l_v, mt_v, c_in, c_all, x, base, pair, loc, part, picked,
    pick, pick_t, same, take, take_t, slot_modes, slot_modes_t, placed_row, wanted_row,
    outer, asked, wanted, send, recv, proj, bring, recv_sem, send_sem, index_sem, proj_sem, coarse_sem,
):
    me = lax.axis_index("wide")
    col = lax.axis_index("narrow")
    at_y, at_z, at_x = me // 8, lax.rem(me // 4, 2), lax.rem(me, 4)
    peers = [
        (lax.rem(at_y + dy, 4) * 2 + lax.rem(at_z + dz, 2)) * 4 + lax.rem(at_x + dx, 4) for dy, dz, dx in OFFSETS
    ]
    barrier = pltpu.get_barrier_semaphore()
    for j in range(SELF):
        pl.semaphore_signal(barrier, inc=1, device_id=(peers[j], col), device_id_type=MESH)
    for d in range(1, ACROSS):
        pl.semaphore_signal(barrier, inc=1, device_id=(me, lax.rem(col + d, ACROSS)), device_id_type=MESH)

    fetch_start = pltpu.make_async_copy(start, x, bring.at[0])
    fetch_coarse = pltpu.make_async_copy(coarse_inverse, c_in, bring.at[1])
    fetch_stiff = pltpu.make_async_copy(stiffness, k_v, bring.at[2])
    fetch_modes = pltpu.make_async_copy(modes_t, mt_v, bring.at[3])
    fetch_local = pltpu.make_async_copy(local_inverse, l_v, bring.at[4])
    fetch_start.start()
    fetch_coarse.start()
    fetch_stiff.start()
    fetch_modes.start()
    fetch_local.start()

    rows = jnp.concatenate([margin_rows[s:s + 1, :] for s in range(SUBS)], axis=1).astype(F32)
    source = jnp.floor((rows + 0.5) * (1.0 / HELD))
    within = rows - source * HELD
    place = lax.broadcasted_iota(jnp.int32, (OWNERS, OUTER), 0)
    owner = jnp.zeros((OWNERS, OUTER), jnp.int32)
    for j in range(OWNERS):
        owner = jnp.where(place == j, peers[j], owner)
    owned = source == owner.astype(F32)
    owned_b = jnp.where(owned, 1.0, 0.0).astype(BF16)

    def earlier(i, _):
        down = (lax.broadcasted_iota(jnp.int32, (STRIP, OUTER), 0) + i * STRIP).astype(F32)
        take[strip(i), :OUTER] = jnp.where(down < iota((STRIP, OUTER), 1), 1.0, 0.0).astype(BF16)
        return 0

    lax.fori_loop(0, OUTER // STRIP, earlier, 0)
    before = dot(owned_b, take[:, :OUTER])
    rank = jnp.sum(jnp.where(owned, before, 0.0), axis=0, keepdims=True)
    placed = jnp.sum(jnp.where(owned, before + CAP * place.astype(F32), 0.0), axis=0, keepdims=True)
    placed_row[...] = placed

    store_column(rank, picked.at[:OUTER])
    ranked = picked[:OUTER, :] == iota((OUTER, STRIP), 1)
    store_column(within + 1.0, picked.at[:OUTER])
    high, low = split_digits(jnp.where(ranked, picked[:OUTER, :], 0.0))
    ask = dot(owned_b, high) * 64.0 + dot(owned_b, low)
    asked[...] = jnp.broadcast_to(ask[:, None, :], (OWNERS, 8, STRIP))

    pl.semaphore_wait(barrier, OWNERS - 1 + ACROSS - 1)

    for j in range(SELF):
        pltpu.make_async_remote_copy(
            asked.at[j], wanted.at[BACK[j]], index_sem.at[0], index_sem.at[1],
            device_id=(peers[j], col), device_id_type=MESH,
        ).start()
    wanted[SELF] = asked[SELF]

    store_column(placed, picked.at[:OUTER])
    fill_by_column(take, picked)
    fill_by_row(take_t, placed_row)

    fetch_start.wait()

    def lower(s, _):
        pair[pl.ds(pl.multiple_of(s * CORE, CORE), CORE), :COLS] = x[pl.ds(pl.multiple_of(s * CORE, CORE), CORE), :].astype(BF16)
        return 0

    lax.fori_loop(0, SUBS, lower, 0)

    for k in range(2):
        pltpu.make_async_copy(wanted.at[pl.ds(0, OWNERS - 1)], wanted.at[pl.ds(0, OWNERS - 1)], index_sem.at[k]).wait()
    slot_of = jnp.max(wanted[...], axis=1)
    high, low = split_digits(slot_of)
    slot = iota((STRIP, SLOTS), 1)
    owner_of = jnp.floor((slot + 0.5) * (1.0 / CAP))
    spread = jnp.where(slot - owner_of * CAP == iota((STRIP, SLOTS), 0), 1.0, 0.0).astype(BF16)
    wide = dot(high, spread) * 64.0 + dot(low, spread)
    row = jnp.sum(jnp.where(owner_of[:OWNERS] == iota((OWNERS, SLOTS), 0), wide, 0.0), axis=0, keepdims=True) - 1.0
    wanted_row[...] = row
    store_column(jnp.where(row < 0.0, -2.0, row), picked)
    fill_by_column(pick, picked)

    def ship(which, i):
        half = which % 2
        for j in range(i * EACH, (i + 1) * EACH):
            if j == SELF:
                recv[which, j] = send[half, j]
            else:
                pltpu.make_async_remote_copy(
                    send.at[half, j], recv.at[which, BACK[j]], send_sem.at[which], recv_sem.at[which],
                    device_id=(peers[j], col), device_id_type=MESH,
                ).start()

    def arrive(which):
        others = recv.at[which, pl.ds(0, OWNERS - 1)]
        pltpu.make_async_copy(others, others, recv_sem.at[which]).wait()
        pltpu.make_async_copy(others, others, send_sem.at[which]).wait()

    def tile(i):
        return pl.ds(pl.multiple_of(i * TILE, TILE), TILE)

    def give(which, i, value):
        send[which % 2, i * EACH:(i + 1) * EACH] = value.astype(BF16).reshape(EACH, CAP, COLS)
        ship(which, i)

    def received(which):
        return recv[which].reshape(SLOTS, COLS)

    def rows_of(s):
        return pl.ds(pl.multiple_of(s * CORE, CORE), CORE)

    def margin_of(s):
        return pl.ds(pl.multiple_of(s * MARGIN, MARGIN), MARGIN)

    def halves(v):
        upper = v.astype(BF16)
        return upper, (v - upper.astype(F32)).astype(BF16)

    def joined(both):
        return both[:, :COLS] + both[:, COLS:]

    def pick_pairs():
        def split(s, _):
            pair[rows_of(s), :COLS], pair[rows_of(s), COLS:] = halves(base[rows_of(s), :])
            return 0

        lax.fori_loop(0, SUBS, split, 0)

        def body(i, _):
            picked[tile(i), :] = joined(dot(pick[tile(i), :], pair[...]))
            return 0

        lax.fori_loop(0, TILES, body, 0)

    def correct_picked(to, which, sign):
        arrived = received(which)
        for i in range(TILES):
            give(to, i, picked[i * TILE:(i + 1) * TILE, :] + sign * dot(same[i * TILE:(i + 1) * TILE, :], arrived))

    for i in range(TILES):
        give(GATHER, i, dot(pick[i * TILE:(i + 1) * TILE, :], pair[:, :COLS]))

    fetch_coarse.wait()
    c_all[pl.ds(col, 1)] = c_in[...].astype(BF16)[None]
    for d in range(1, ACROSS):
        pltpu.make_async_remote_copy(
            c_all.at[col], c_all.at[col], coarse_sem.at[0], coarse_sem.at[1],
            device_id=(me, lax.rem(col + d, ACROSS)), device_id_type=MESH,
        ).start()

    fill_equal(same, picked, wanted_row)
    fill_by_row(pick_t, wanted_row)

    fetch_modes.wait()
    slot_modes_t[:, :OUTER] = jnp.zeros((COARSE, OUTER), BF16)
    for s in range(SUBS):
        slot_modes_t[s * MODES:(s + 1) * MODES, s * MARGIN:(s + 1) * MARGIN] = mt_v[s, :, CORE:]
    unit = jnp.where(iota((STRIP, STRIP), 0) == iota((STRIP, STRIP), 1), 1.0, 0.0).astype(BF16)
    for k in range(OUTER // STRIP):
        outer[k * STRIP:(k + 1) * STRIP, :] = lax.dot_general(
            unit, slot_modes_t[:, k * STRIP:(k + 1) * STRIP], (((1,), (1,)), ((), ())), preferred_element_type=F32
        ).astype(BF16)
    slot_modes[...] = dot(take_t[...], outer[...]).astype(BF16)
    slot_modes_t[...] = dot(slot_modes_t[:, :OUTER], take[...]).astype(BF16)
    fetch_stiff.wait()

    def iteration(it, _):
        fetch_loads = pltpu.make_async_copy(loads, base, bring.at[5])
        fetch_loads.start()

        def from_core(s, _):
            loc[s, :CORE, :] = x[rows_of(s), :].astype(BF16)
            part[s] = dot(k_v[s, :, :CORE], loc[s, :CORE, :])
            return 0

        lax.fori_loop(0, SUBS, from_core, 0)
        arrive(GATHER)
        arrived = received(GATHER)
        for s in range(SUBS):
            near = slice(s * MARGIN, (s + 1) * MARGIN)
            margin = dot(take[near, :], arrived).astype(BF16)
            loc[s, CORE:, :] = margin
            outer[near, :] = (part[s, CORE:, :] + dot(k_v[s, CORE:, CORE:], margin)).astype(BF16)
        for i in range(TILES):
            give(SCATTER, i, dot(take_t[i * TILE:(i + 1) * TILE, :], outer[...]))
        fetch_loads.wait()

        def core_part(s, _):
            base[rows_of(s), :] = base[rows_of(s), :] - (part[s, :CORE, :] + dot(k_v[s, :CORE, CORE:], loc[s, CORE:, :]))
            return 0

        lax.fori_loop(0, SUBS, core_part, 0)

        @pl.when(it < ITERS)
        def _():
            pick_pairs()

        arrive(SCATTER)

        @pl.when(it < ITERS)
        def _():
            correct_picked(REGATHER, SCATTER, -1.0)

        def finish_residual(s, _):
            base[rows_of(s), :] = base[rows_of(s), :] - dot(pick_t[rows_of(s), :], received(SCATTER))
            return 0

        lax.fori_loop(0, SUBS, finish_residual, 0)

        @pl.when(it < ITERS)
        def _():
            @pl.when(it == 0)
            def _():
                fetch_local.wait()
                for k in range(2):
                    pltpu.make_async_copy(c_all.at[pl.ds(0, 3)], c_all.at[pl.ds(0, 3)], coarse_sem.at[k]).wait()

            def solve_core(s, _):
                loc[s, :CORE, :] = base[rows_of(s), :].astype(BF16)
                part[s] = dot(l_v[s, :, :CORE], loc[s, :CORE, :])
                return 0

            lax.fori_loop(0, SUBS, solve_core, 0)
            projected = jnp.concatenate([dot(mt_v[s, :, :CORE], loc[s, :CORE, :]) for s in range(SUBS)], axis=0)
            arrive(REGATHER)
            proj[pl.ds(me, 1)] = (projected + dot(slot_modes_t[...], received(REGATHER))).astype(BF16)[None]
            for j in range(SELF):
                pltpu.make_async_remote_copy(
                    proj.at[me], proj.at[me], proj_sem.at[0], proj_sem.at[1],
                    device_id=(peers[j], col), device_id_type=MESH,
                ).start()

            def solve_margin(s, _):
                margin = dot(take[margin_of(s), :], received(REGATHER)).astype(BF16)
                whole = part[s] + dot(l_v[s, :, CORE:], margin)
                base[rows_of(s), :] = x[rows_of(s), :] + 0.5 * whole[:CORE]
                pair[margin_of(s), :COLS], pair[margin_of(s), COLS:] = halves(0.5 * whole[CORE:])
                return 0

            lax.fori_loop(0, SUBS, solve_margin, 0)

            def in_slots(i, _):
                picked[tile(i), :] = joined(dot(take_t[tile(i), :], pair[:OUTER, :]))
                return 0

            lax.fori_loop(0, TILES, in_slots, 0)
            for k in range(2):
                pltpu.make_async_copy(
                    proj.at[pl.ds(0, OWNERS - 1)], proj.at[pl.ds(0, OWNERS - 1)], proj_sem.at[k]
                ).wait()
            per = WIDTH // COARSE
            coarse = dot(c_all[0], proj[:per].reshape(WIDTH, COLS))
            for n in range(1, ACROSS):
                coarse = coarse + dot(c_all[n], proj[n * per:(n + 1) * per].reshape(WIDTH, COLS))
            coarse = jnp.concatenate(halves(coarse), axis=1)
            for i in range(TILES):
                lifted = joined(dot(slot_modes[i * TILE:(i + 1) * TILE, :], coarse))
                give(CORRECT, i, picked[i * TILE:(i + 1) * TILE, :] + lifted)
            for s in range(SUBS):
                lifted = lax.dot_general(
                    mt_v[s, :, :CORE], coarse[s * MODES:(s + 1) * MODES], (((0,), (0,)), ((), ())),
                    preferred_element_type=F32,
                )
                base[s * CORE:(s + 1) * CORE, :] = base[s * CORE:(s + 1) * CORE, :] + joined(lifted)
            pick_pairs()
            arrive(CORRECT)
            correct_picked(GATHER, CORRECT, 1.0)

            def finish_step(s, _):
                x[rows_of(s), :] = base[rows_of(s), :] + dot(pick_t[rows_of(s), :], received(CORRECT))
                return 0

            lax.fori_loop(0, SUBS, finish_step, 0)

        return 0

    lax.fori_loop(0, ITERS + 1, iteration, 0)
    give_x = pltpu.make_async_copy(x, out_x, bring.at[6])
    give_r = pltpu.make_async_copy(base, out_r, bring.at[7])
    give_x.start()
    give_r.start()
    give_x.wait()
    give_r.wait()


def shards(loads, start, stiffness, local_inverse, modes, coarse_inverse, margin_rows):
    field = jax.ShapeDtypeStruct((HELD, COLS), F32)
    hbm = pl.BlockSpec(memory_space=pl.ANY)
    return pl.pallas_call(
        kernel,
        out_shape=(field, field),
        in_specs=[hbm] * 6 + [pl.BlockSpec(memory_space=pltpu.VMEM)],
        out_specs=(hbm, hbm),
        scratch_shapes=[
            pltpu.VMEM((SUBS, ORDER, ORDER), BF16),
            pltpu.VMEM((SUBS, ORDER, ORDER), BF16),
            pltpu.VMEM((SUBS, MODES, ORDER), BF16),
            pltpu.VMEM((COARSE, WIDTH), F32),
            pltpu.VMEM((ACROSS, COARSE, WIDTH), BF16),
            pltpu.VMEM((HELD, COLS), F32),
            pltpu.VMEM((HELD, COLS), F32),
            pltpu.VMEM((HELD, 2 * COLS), BF16),
            pltpu.VMEM((SUBS, ORDER, COLS), BF16),
            pltpu.VMEM((SUBS, ORDER, COLS), F32),
            pltpu.VMEM((SLOTS, COLS), F32),
            pltpu.VMEM((SLOTS, HELD), BF16),
            pltpu.VMEM((HELD, SLOTS), BF16),
            pltpu.VMEM((SLOTS, SLOTS), BF16),
            pltpu.VMEM((OUTER, SLOTS), BF16),
            pltpu.VMEM((SLOTS, OUTER), BF16),
            pltpu.VMEM((SLOTS, COARSE), BF16),
            pltpu.VMEM((COARSE, SLOTS), BF16),
            pltpu.VMEM((1, OUTER), F32),
            pltpu.VMEM((1, SLOTS), F32),
            pltpu.VMEM((OUTER, COLS), BF16),
            pltpu.VMEM((OWNERS, 8, STRIP), F32),
            pltpu.VMEM((OWNERS, 8, STRIP), F32),
            pltpu.VMEM((2, OWNERS, CAP, COLS), BF16),
            pltpu.VMEM((4, OWNERS, CAP, COLS), BF16),
            pltpu.VMEM((OWNERS, COARSE, COLS), BF16),
            pltpu.SemaphoreType.DMA((8,)),
            pltpu.SemaphoreType.DMA((4,)),
            pltpu.SemaphoreType.DMA((4,)),
            pltpu.SemaphoreType.DMA((2,)),
            pltpu.SemaphoreType.DMA((2,)),
            pltpu.SemaphoreType.DMA((2,)),
        ],
        compiler_params=pltpu.CompilerParams(
            collective_id=0, has_side_effects=True, vmem_limit_bytes=63 * 1024 * 1024
        ),
    )(loads, start, stiffness, local_inverse, jnp.swapaxes(modes, 1, 2), coarse_inverse, margin_rows)


def solution(mesh):
    placed = (
        P("wide", "narrow"),
        P("wide", "narrow"),
        P("wide", None, None),
        P("wide", None, None),
        P("wide", None, None),
        P("wide", "narrow"),
        P("wide", None),
    )
    return jax.shard_map(
        shards,
        mesh=mesh,
        in_specs=placed,
        out_specs=(P("wide", "narrow"), P("wide", "narrow")),
        check_vma=False,
    )
```

```python
import jax
import jax.numpy as jnp
from jax import lax
from jax.experimental import pallas as pl
from jax.experimental.pallas import tpu as pltpu
from jax.sharding import PartitionSpec as P

MESH = pl.DeviceIdType.MESH
ITERS = 2
SUBS = 4
ORDER = 1024
TILE = 384
CORE = 768
MARGIN = ORDER - CORE
COLS = 128
MODES = 32
HELD = SUBS * CORE
OUTER = SUBS * MARGIN
OWNERS = 32
ACROSS = 4
CAP = 48
SLOTS = OWNERS * CAP
TILES = SLOTS // TILE
EACH = TILE // CAP
COARSE = SUBS * MODES
WIDTH = 1024
STRIP = 128
F32 = jnp.float32
BF16 = jnp.bfloat16
GATHER, SCATTER, REGATHER, CORRECT = 0, 1, 2, 3
SIDES = (4, 2, 4)


def reach(offset):
    return sum(min(o, n - o) for o, n in zip(offset, SIDES))


OFFSETS = sorted(
    [(dy, dz, dx) for dy in range(SIDES[0]) for dz in range(SIDES[1]) for dx in range(SIDES[2])],
    key=reach, reverse=True,
)
BACK = [OFFSETS.index(tuple((n - o) % n for o, n in zip(offset, SIDES))) for offset in OFFSETS]
SELF = OWNERS - 1


def dot(a, b):
    return jnp.dot(a, b, preferred_element_type=F32)


def iota(shape, axis):
    return lax.broadcasted_iota(jnp.int32, shape, axis).astype(F32)


def strip(i):
    return pl.ds(pl.multiple_of(i * STRIP, STRIP), STRIP)


def split_digits(v):
    high = jnp.floor(v * (1.0 / 64.0))
    return high.astype(BF16), (v - high * 64.0).astype(BF16)


def store_column(row, ref):
    same = iota((STRIP, STRIP), 0) == iota((STRIP, STRIP), 1)
    for k in range(row.shape[1] // STRIP):
        piece = jnp.broadcast_to(row[:, k * STRIP:(k + 1) * STRIP], (STRIP, STRIP))
        column = jnp.sum(jnp.where(same, piece, 0.0), axis=1, keepdims=True)
        ref[k * STRIP:(k + 1) * STRIP, :] = jnp.broadcast_to(column, (STRIP, STRIP))


def fill_by_column(out, column, first, last):
    width = out.shape[1]

    def body(i, _):
        held = column[strip(i), :]
        lanes = iota((STRIP, STRIP), 1)
        for k in range(width // STRIP):
            out[strip(i), k * STRIP:(k + 1) * STRIP] = jnp.where(held == lanes + float(k * STRIP), 1.0, 0.0).astype(BF16)
        return 0

    lax.fori_loop(first, last, body, 0)


def fill_by_row(out, row):
    rows, width = out.shape

    def body(i, _):
        down = (lax.broadcasted_iota(jnp.int32, (STRIP, STRIP), 0) + i * STRIP).astype(F32)
        for k in range(width // STRIP):
            out[strip(i), k * STRIP:(k + 1) * STRIP] = jnp.where(down == row[:, k * STRIP:(k + 1) * STRIP], 1.0, 0.0).astype(BF16)
        return 0

    lax.fori_loop(0, rows // STRIP, body, 0)


def fill_equal(out, column, row):
    rows, width = out.shape

    def body(i, _):
        held = column[strip(i), :]
        for k in range(width // STRIP):
            out[strip(i), k * STRIP:(k + 1) * STRIP] = jnp.where(held == row[:, k * STRIP:(k + 1) * STRIP], 1.0, 0.0).astype(BF16)
        return 0

    lax.fori_loop(0, rows // STRIP, body, 0)


def kernel(
    loads, start, stiffness, local_inverse, modes_t, coarse_inverse, margin_rows,
    out_x, out_r,
    k_v, l_v, mt_v, c_all, x, base, pair, loc, part, picked,
    pick, pick_t, same, near, take, take_t, slot_modes, slot_modes_t, placed_row, wanted_row,
    wanted, send, recv, proj, bring, recv_sem, send_sem, index_sem, proj_sem, coarse_sem,
):
    me = lax.axis_index("wide")
    col = lax.axis_index("narrow")
    at_y, at_z, at_x = me // 8, lax.rem(me // 4, 2), lax.rem(me, 4)
    peers = [
        (lax.rem(at_y + dy, 4) * 2 + lax.rem(at_z + dz, 2)) * 4 + lax.rem(at_x + dx, 4) for dy, dz, dx in OFFSETS
    ]
    barrier = pltpu.get_barrier_semaphore()
    for j in range(SELF):
        pl.semaphore_signal(barrier, inc=1, device_id=(peers[j], col), device_id_type=MESH)
    for d in range(1, ACROSS):
        pl.semaphore_signal(barrier, inc=1, device_id=(me, lax.rem(col + d, ACROSS)), device_id_type=MESH)

    fetch_start = pltpu.make_async_copy(start, x, bring.at[0])
    fetch_stiff = pltpu.make_async_copy(stiffness, k_v, bring.at[2])
    fetch_modes = pltpu.make_async_copy(modes_t, mt_v, bring.at[3])
    fetch_local = pltpu.make_async_copy(local_inverse, l_v, bring.at[4])
    fetch_start.start()
    for k in range(WIDTH // STRIP):
        pltpu.make_async_copy(
            coarse_inverse.at[:, k * STRIP:(k + 1) * STRIP], base.at[k * STRIP:(k + 1) * STRIP], bring.at[1]
        ).start()
    fetch_stiff.start()
    fetch_modes.start()
    fetch_local.start()

    rows = jnp.concatenate([margin_rows[s:s + 1, :] for s in range(SUBS)], axis=1).astype(F32)
    source = jnp.floor((rows + 0.5) * (1.0 / HELD))
    within = rows - source * HELD
    place = lax.broadcasted_iota(jnp.int32, (OWNERS, OUTER), 0)
    owner = jnp.zeros((OWNERS, OUTER), jnp.int32)
    for j in range(OWNERS):
        owner = jnp.where(place == j, peers[j], owner)
    owned = source == owner.astype(F32)
    owned_b = jnp.where(owned, 1.0, 0.0).astype(BF16)

    def earlier(i, _):
        down = (lax.broadcasted_iota(jnp.int32, (STRIP, OUTER), 0) + i * STRIP).astype(F32)
        take[strip(i), :OUTER] = jnp.where(down < iota((STRIP, OUTER), 1), 1.0, 0.0).astype(BF16)
        return 0

    lax.fori_loop(0, OUTER // STRIP, earlier, 0)
    before = dot(owned_b, take[:, :OUTER])
    rank = jnp.sum(jnp.where(owned, before, 0.0), axis=0, keepdims=True)
    placed = jnp.sum(jnp.where(owned, before + CAP * place.astype(F32), 0.0), axis=0, keepdims=True)
    placed_row[...] = placed

    store_column(rank, picked.at[:OUTER])
    ranked = picked[:OUTER, :] == iota((OUTER, STRIP), 1)
    store_column(within + 1.0, picked.at[:OUTER])
    high, low = split_digits(jnp.where(ranked, picked[:OUTER, :], 0.0))
    ask = dot(owned_b, high) * 64.0 + dot(owned_b, low)
    part[0, :OWNERS * 8, :] = jnp.broadcast_to(ask[:, None, :], (OWNERS, 8, STRIP)).reshape(OWNERS * 8, STRIP)

    pl.semaphore_wait(barrier, OWNERS - 1 + ACROSS - 1)

    for j in range(SELF):
        pltpu.make_async_remote_copy(
            part.at[0, j * 8:(j + 1) * 8], wanted.at[BACK[j]], index_sem.at[0], index_sem.at[1],
            device_id=(peers[j], col), device_id_type=MESH,
        ).start()
    wanted[SELF] = part[0, SELF * 8:OWNERS * 8, :]

    store_column(placed, picked.at[:OUTER])
    fill_by_column(take, picked, 0, OUTER // STRIP)
    fill_by_row(take_t, placed_row)

    fetch_start.wait()

    def lower(s, _):
        pair[pl.ds(pl.multiple_of(s * CORE, CORE), CORE), :COLS] = x[pl.ds(pl.multiple_of(s * CORE, CORE), CORE), :].astype(BF16)
        return 0

    lax.fori_loop(0, SUBS, lower, 0)

    fetch_modes.wait()
    slot_modes_t[:, :OUTER] = jnp.zeros((COARSE, OUTER), BF16)
    for s in range(SUBS):
        slot_modes_t[s * MODES:(s + 1) * MODES, s * MARGIN:(s + 1) * MARGIN] = mt_v[s, :, CORE:]
    unit = jnp.where(iota((STRIP, STRIP), 0) == iota((STRIP, STRIP), 1), 1.0, 0.0).astype(BF16)
    for k in range(OUTER // STRIP):
        pair[k * STRIP:(k + 1) * STRIP, COLS:] = lax.dot_general(
            unit, slot_modes_t[:, k * STRIP:(k + 1) * STRIP], (((1,), (1,)), ((), ())), preferred_element_type=F32
        ).astype(BF16)
    slot_modes[...] = dot(take_t[...], pair[:OUTER, COLS:]).astype(BF16)
    slot_modes_t[...] = dot(slot_modes_t[:, :OUTER], take[...]).astype(BF16)

    for k in range(2):
        pltpu.make_async_copy(wanted.at[pl.ds(0, OWNERS - 1)], wanted.at[pl.ds(0, OWNERS - 1)], index_sem.at[k]).wait()
    slot_of = jnp.max(wanted[...], axis=1)
    high, low = split_digits(slot_of)
    slot = iota((STRIP, SLOTS), 1)
    owner_of = jnp.floor((slot + 0.5) * (1.0 / CAP))
    spread = jnp.where(slot - owner_of * CAP == iota((STRIP, SLOTS), 0), 1.0, 0.0).astype(BF16)
    wide = dot(high, spread) * 64.0 + dot(low, spread)
    row = jnp.sum(jnp.where(owner_of[:OWNERS] == iota((OWNERS, SLOTS), 0), wide, 0.0), axis=0, keepdims=True) - 1.0
    wanted_row[...] = row
    store_column(jnp.where(row < 0.0, -2.0, row), picked)

    def ship(which, i):
        half = which % 2
        for j in range(i * EACH, (i + 1) * EACH):
            if j == SELF:
                recv[which, j] = send[half, j]
            else:
                pltpu.make_async_remote_copy(
                    send.at[half, j], recv.at[which, BACK[j]], send_sem.at[which], recv_sem.at[which, BACK[j] // EACH],
                    device_id=(peers[j], col), device_id_type=MESH,
                ).start()

    def arrive(which, k):
        first, last = k * EACH, min((k + 1) * EACH, SELF)
        blocks = recv.at[which, first:last]
        pltpu.make_async_copy(blocks, blocks, recv_sem.at[which, k]).wait()
        if k == 0:
            others = recv.at[which, :SELF]
            pltpu.make_async_copy(others, others, send_sem.at[which]).wait()
        return recv[which, k * EACH:(k + 1) * EACH].reshape(TILE, COLS)

    def tile(i):
        return pl.ds(pl.multiple_of(i * TILE, TILE), TILE)

    def give(which, i, value):
        send[which % 2, i * EACH:(i + 1) * EACH] = value.astype(BF16).reshape(EACH, CAP, COLS)
        ship(which, i)

    def received(which):
        return recv[which].reshape(SLOTS, COLS)

    def rows_of(s):
        return pl.ds(pl.multiple_of(s * CORE, CORE), CORE)

    def margin_of(s):
        return pl.ds(pl.multiple_of(s * MARGIN, MARGIN), MARGIN)

    def halves(v):
        upper = v.astype(BF16)
        return upper, (v - upper.astype(F32)).astype(BF16)

    def joined(both):
        return both[:, :COLS] + both[:, COLS:]

    def pick_pairs():
        def split(s, _):
            pair[rows_of(s), :COLS], pair[rows_of(s), COLS:] = halves(base[rows_of(s), :])
            return 0

        lax.fori_loop(0, SUBS, split, 0)

        def body(i, _):
            picked[tile(i), :] = joined(dot(pick[tile(i), :], pair[...]))
            return 0

        lax.fori_loop(0, TILES, body, 0)

    def answer(to, which, table, sign):
        for k in reversed(range(TILES)):
            arrived = arrive(which, k)
            for i in range(TILES):
                rows = slice(i * TILE, (i + 1) * TILE)
                value = picked[rows, :] + sign * dot(table[rows, k * TILE:(k + 1) * TILE], arrived)
                if k > 0:
                    picked[rows, :] = value
                else:
                    give(to, i, value)

    for i in range(TILES):
        fill_by_column(pick, picked, i * TILE // STRIP, (i + 1) * TILE // STRIP)
        give(GATHER, i, dot(pick[i * TILE:(i + 1) * TILE, :], pair[:, :COLS]))

    pltpu.make_async_copy(base.at[:WIDTH], base.at[:WIDTH], bring.at[1]).wait()
    for k in range(WIDTH // STRIP):
        c_all[col, :, k * STRIP:(k + 1) * STRIP] = base[k * STRIP:(k + 1) * STRIP, :].astype(BF16)
    for d in range(1, ACROSS):
        pltpu.make_async_remote_copy(
            c_all.at[col], c_all.at[col], coarse_sem.at[0], coarse_sem.at[1],
            device_id=(me, lax.rem(col + d, ACROSS)), device_id_type=MESH,
        ).start()

    fill_equal(same, picked, wanted_row)
    fetch_stiff.wait()

    def order(c, _):
        lanes = pl.ds(pl.multiple_of(c * 2 * COLS, 2 * COLS), 2 * COLS)
        for s in range(SUBS):
            rows = slice(s * MARGIN, (s + 1) * MARGIN)
            pair[rows, :] = dot(k_v[s, CORE:, CORE:], take[rows, lanes]).astype(BF16)
        for i in range(TILES):
            rows = slice(i * TILE, (i + 1) * TILE)
            near[rows, lanes] = dot(take_t[rows, :], pair[:OUTER, :]).astype(BF16)
        return 0

    lax.fori_loop(0, SLOTS // (2 * COLS), order, 0)

    def in_slots(i, _):
        picked[tile(i), :] = joined(dot(take_t[tile(i), :], pair[:OUTER, :]))
        return 0

    give_x = pltpu.make_async_copy(x, out_x, bring.at[6])

    def iteration(it, _):
        fetch_loads = pltpu.make_async_copy(loads, base, bring.at[5])
        fetch_loads.start()

        def from_core(s, _):
            loc[s, :CORE, :] = x[rows_of(s), :].astype(BF16)
            part[s] = dot(k_v[s, :, :CORE], loc[s, :CORE, :])
            pair[margin_of(s), :COLS], pair[margin_of(s), COLS:] = halves(part[s, CORE:, :])
            return 0

        lax.fori_loop(0, SUBS, from_core, 0)
        lax.fori_loop(0, TILES, in_slots, 0)

        @pl.when(it == ITERS)
        def _():
            give_x.start()

        answer(SCATTER, GATHER, near, 1.0)
        fetch_loads.wait()

        def core_part(s, _):
            margin = dot(take[margin_of(s), :], received(GATHER)).astype(BF16)
            base[rows_of(s), :] = base[rows_of(s), :] - (part[s, :CORE, :] + dot(k_v[s, :CORE, CORE:], margin))
            return 0

        lax.fori_loop(0, SUBS, core_part, 0)

        @pl.when(it < ITERS)
        def _():
            pick_pairs()
            answer(REGATHER, SCATTER, same, -1.0)

        @pl.when(it == ITERS)
        def _():
            for k in reversed(range(TILES)):
                arrive(SCATTER, k)

        @pl.when(it == 0)
        def _():
            fill_by_row(pick_t, wanted_row)

        def finish_residual(s, _):
            base[rows_of(s), :] = base[rows_of(s), :] - dot(pick_t[rows_of(s), :], received(SCATTER))

            @pl.when(it == ITERS)
            def _():
                pltpu.make_async_copy(base.at[rows_of(s)], out_r.at[rows_of(s)], bring.at[7]).start()

            return 0

        lax.fori_loop(0, SUBS, finish_residual, 0)

        @pl.when(it < ITERS)
        def _():
            @pl.when(it == 0)
            def _():
                fetch_local.wait()
                for k in range(2):
                    pltpu.make_async_copy(c_all.at[pl.ds(0, 3)], c_all.at[pl.ds(0, 3)], coarse_sem.at[k]).wait()

            def solve_core(s, _):
                loc[s, :CORE, :] = base[rows_of(s), :].astype(BF16)
                part[s] = dot(l_v[s, :, :CORE], loc[s, :CORE, :])
                return 0

            lax.fori_loop(0, SUBS, solve_core, 0)
            projected = jnp.concatenate([dot(mt_v[s, :, :CORE], loc[s, :CORE, :]) for s in range(SUBS)], axis=0)
            for k in reversed(range(TILES)):
                projected = projected + dot(slot_modes_t[:, k * TILE:(k + 1) * TILE], arrive(REGATHER, k))
            proj[pl.ds(me, 1)] = projected.astype(BF16)[None]
            for j in range(SELF):
                pltpu.make_async_remote_copy(
                    proj.at[me], proj.at[me], proj_sem.at[0], proj_sem.at[1],
                    device_id=(peers[j], col), device_id_type=MESH,
                ).start()

            def solve_margin(s, _):
                margin = dot(take[margin_of(s), :], received(REGATHER)).astype(BF16)
                whole = part[s] + dot(l_v[s, :, CORE:], margin)
                base[rows_of(s), :] = x[rows_of(s), :] + 0.5 * whole[:CORE]
                pair[margin_of(s), :COLS], pair[margin_of(s), COLS:] = halves(0.5 * whole[CORE:])
                return 0

            lax.fori_loop(0, SUBS, solve_margin, 0)

            lax.fori_loop(0, TILES, in_slots, 0)
            for k in range(2):
                pltpu.make_async_copy(
                    proj.at[pl.ds(0, OWNERS - 1)], proj.at[pl.ds(0, OWNERS - 1)], proj_sem.at[k]
                ).wait()
            per = WIDTH // COARSE
            coarse = dot(c_all[0], proj[:per].reshape(WIDTH, COLS))
            for n in range(1, ACROSS):
                coarse = coarse + dot(c_all[n], proj[n * per:(n + 1) * per].reshape(WIDTH, COLS))
            coarse = jnp.concatenate(halves(coarse), axis=1)
            for i in range(TILES):
                lifted = joined(dot(slot_modes[i * TILE:(i + 1) * TILE, :], coarse))
                give(CORRECT, i, picked[i * TILE:(i + 1) * TILE, :] + lifted)
            for s in range(SUBS):
                lifted = lax.dot_general(
                    mt_v[s, :, :CORE], coarse[s * MODES:(s + 1) * MODES], (((0,), (0,)), ((), ())),
                    preferred_element_type=F32,
                )
                base[s * CORE:(s + 1) * CORE, :] = base[s * CORE:(s + 1) * CORE, :] + joined(lifted)
            pick_pairs()
            answer(GATHER, CORRECT, same, 1.0)

            def finish_step(s, _):
                x[rows_of(s), :] = base[rows_of(s), :] + dot(pick_t[rows_of(s), :], received(CORRECT))
                return 0

            lax.fori_loop(0, SUBS, finish_step, 0)

        return 0

    lax.fori_loop(0, ITERS + 1, iteration, 0)
    give_x.wait()
    pltpu.make_async_copy(base, out_r, bring.at[7]).wait()


def shards(loads, start, stiffness, local_inverse, modes, coarse_inverse, margin_rows):
    field = jax.ShapeDtypeStruct((HELD, COLS), F32)
    hbm = pl.BlockSpec(memory_space=pl.ANY)
    return pl.pallas_call(
        kernel,
        out_shape=(field, field),
        in_specs=[hbm] * 6 + [pl.BlockSpec(memory_space=pltpu.VMEM)],
        out_specs=(hbm, hbm),
        scratch_shapes=[
            pltpu.VMEM((SUBS, ORDER, ORDER), BF16),
            pltpu.VMEM((SUBS, ORDER, ORDER), BF16),
            pltpu.VMEM((SUBS, MODES, ORDER), BF16),
            pltpu.VMEM((ACROSS, COARSE, WIDTH), BF16),
            pltpu.VMEM((HELD, COLS), F32),
            pltpu.VMEM((HELD, COLS), F32),
            pltpu.VMEM((HELD, 2 * COLS), BF16),
            pltpu.VMEM((SUBS, ORDER, COLS), BF16),
            pltpu.VMEM((SUBS, ORDER, COLS), F32),
            pltpu.VMEM((SLOTS, COLS), F32),
            pltpu.VMEM((SLOTS, HELD), BF16),
            pltpu.VMEM((HELD, SLOTS), BF16),
            pltpu.VMEM((SLOTS, SLOTS), BF16),
            pltpu.VMEM((SLOTS, SLOTS), BF16),
            pltpu.VMEM((OUTER, SLOTS), BF16),
            pltpu.VMEM((SLOTS, OUTER), BF16),
            pltpu.VMEM((SLOTS, COARSE), BF16),
            pltpu.VMEM((COARSE, SLOTS), BF16),
            pltpu.VMEM((1, OUTER), F32),
            pltpu.VMEM((1, SLOTS), F32),
            pltpu.VMEM((OWNERS, 8, STRIP), F32),
            pltpu.VMEM((2, OWNERS, CAP, COLS), BF16),
            pltpu.VMEM((4, OWNERS, CAP, COLS), BF16),
            pltpu.VMEM((OWNERS, COARSE, COLS), BF16),
            pltpu.SemaphoreType.DMA((8,)),
            pltpu.SemaphoreType.DMA((4, TILES)),
            pltpu.SemaphoreType.DMA((4,)),
            pltpu.SemaphoreType.DMA((2,)),
            pltpu.SemaphoreType.DMA((2,)),
            pltpu.SemaphoreType.DMA((2,)),
        ],
        compiler_params=pltpu.CompilerParams(
            collective_id=0, has_side_effects=True, vmem_limit_bytes=64 * 1024 * 1024
        ),
    )(loads, start, stiffness, local_inverse, jnp.swapaxes(modes, 1, 2), coarse_inverse, margin_rows)


def solution(mesh):
    placed = (
        P("wide", "narrow"),
        P("wide", "narrow"),
        P("wide", None, None),
        P("wide", None, None),
        P("wide", None, None),
        P("wide", "narrow"),
        P("wide", None),
    )
    return jax.shard_map(
        shards,
        mesh=mesh,
        in_specs=placed,
        out_specs=(P("wide", "narrow"), P("wide", "narrow")),
        check_vma=False,
    )
```

```python
import jax
import jax.numpy as jnp
from jax import lax
from jax.experimental import pallas as pl
from jax.experimental.pallas import tpu as pltpu
from jax.sharding import PartitionSpec as P

MESH = pl.DeviceIdType.MESH
ITERS = 2
SUBS = 4
ORDER = 1024
TILE = 384
CORE = 768
MARGIN = ORDER - CORE
COLS = 128
MODES = 32
HELD = SUBS * CORE
OUTER = SUBS * MARGIN
OWNERS = 32
ACROSS = 4
CAP = 48
SLOTS = OWNERS * CAP
TILES = SLOTS // TILE
EACH = TILE // CAP
COARSE = SUBS * MODES
WIDTH = 1024
STRIP = 128
ROWS_Y = 4
PLANE = 8
F32 = jnp.float32
BF16 = jnp.bfloat16
GATHER, SCATTER, REGATHER, CORRECT = 0, 1, 2, 3
SIDES = (4, 2, 4)


def reach(offset):
    return sum(min(o, n - o) for o, n in zip(offset, SIDES))


OFFSETS = sorted(
    [(dy, dz, dx) for dy in range(SIDES[0]) for dz in range(SIDES[1]) for dx in range(SIDES[2])],
    key=reach, reverse=True,
)
BACK = [OFFSETS.index(tuple((n - o) % n for o, n in zip(offset, SIDES))) for offset in OFFSETS]
SELF = OWNERS - 1


def dot(a, b):
    return jnp.dot(a, b, preferred_element_type=F32)


def iota(shape, axis):
    return lax.broadcasted_iota(jnp.int32, shape, axis).astype(F32)


def strip(i):
    return pl.ds(pl.multiple_of(i * STRIP, STRIP), STRIP)


def split_digits(v):
    high = jnp.floor(v * (1.0 / 64.0))
    return high.astype(BF16), (v - high * 64.0).astype(BF16)


def store_column(row, ref):
    same = iota((STRIP, STRIP), 0) == iota((STRIP, STRIP), 1)
    for k in range(row.shape[1] // STRIP):
        piece = jnp.broadcast_to(row[:, k * STRIP:(k + 1) * STRIP], (STRIP, STRIP))
        column = jnp.sum(jnp.where(same, piece, 0.0), axis=1, keepdims=True)
        ref[k * STRIP:(k + 1) * STRIP, :] = jnp.broadcast_to(column, (STRIP, STRIP))


def fill_by_column(out, column):
    rows, width = out.shape

    def body(i, _):
        held = column[strip(i), :]
        lanes = iota((STRIP, STRIP), 1)
        for k in range(width // STRIP):
            out[strip(i), k * STRIP:(k + 1) * STRIP] = jnp.where(held == lanes + float(k * STRIP), 1.0, 0.0).astype(BF16)
        return 0

    lax.fori_loop(0, rows // STRIP, body, 0)


def fill_by_row(out, row):
    rows, width = out.shape

    def body(i, _):
        down = (lax.broadcasted_iota(jnp.int32, (STRIP, STRIP), 0) + i * STRIP).astype(F32)
        for k in range(width // STRIP):
            out[strip(i), k * STRIP:(k + 1) * STRIP] = jnp.where(down == row[:, k * STRIP:(k + 1) * STRIP], 1.0, 0.0).astype(BF16)
        return 0

    lax.fori_loop(0, rows // STRIP, body, 0)


def fill_equal(out, column, row):
    rows, width = out.shape

    def body(i, _):
        held = column[strip(i), :]
        for k in range(width // STRIP):
            out[strip(i), k * STRIP:(k + 1) * STRIP] = jnp.where(held == row[:, k * STRIP:(k + 1) * STRIP], 1.0, 0.0).astype(BF16)
        return 0

    lax.fori_loop(0, rows // STRIP, body, 0)


def kernel(
    loads, start, stiffness, local_inverse, modes_t, coarse_inverse, margin_rows,
    out_x, out_r,
    k_v, l_v, mt_v, tile_t, block, x, base, pair, loc, part, picked,
    pick, pick_t, same, take, take_t, slot_modes, slot_modes_t, placed_row, wanted_row,
    outer, asked, wanted, send, recv, proj, bits, sums, bring, recv_sem, send_sem, index_sem, proj_sem, sum_sem, coarse_sem,
):
    me = lax.axis_index("wide")
    col = lax.axis_index("narrow")
    at_y, at_z, at_x = me // 8, lax.rem(me // 4, 2), lax.rem(me, 4)
    peers = [
        (lax.rem(at_y + dy, 4) * 2 + lax.rem(at_z + dz, 2)) * 4 + lax.rem(at_x + dx, 4) for dy, dz, dx in OFFSETS
    ]
    barrier = pltpu.get_barrier_semaphore()
    for j in range(SELF):
        pl.semaphore_signal(barrier, inc=1, device_id=(peers[j], col), device_id_type=MESH)
    at_q = lax.rem(me, PLANE)
    stays = col == at_y
    takers = [(col * PLANE + at_q, lax.rem(col + d, ACROSS)) for d in range(ACROSS)]
    for d in range(1, ACROSS):
        pl.semaphore_signal(barrier, inc=1, device_id=takers[d], device_id_type=MESH)

    @pl.when(jnp.logical_not(stays))
    def _():
        for d in range(1, ROWS_Y):
            giver = (lax.rem(col + d, ROWS_Y) * PLANE + at_q, at_y)
            pl.semaphore_signal(barrier, inc=1, device_id=giver, device_id_type=MESH)

    fetch_start = pltpu.make_async_copy(start, x, bring.at[0])
    fetch_stiff = pltpu.make_async_copy(stiffness, k_v, bring.at[2])
    fetch_modes = pltpu.make_async_copy(modes_t, mt_v, bring.at[3])
    fetch_local = pltpu.make_async_copy(local_inverse, l_v, bring.at[4])
    fetch_start.start()
    for k in range(WIDTH // STRIP):
        pltpu.make_async_copy(
            coarse_inverse.at[:, k * STRIP:(k + 1) * STRIP], base.at[k * STRIP:(k + 1) * STRIP], bring.at[1]
        ).start()
    fetch_stiff.start()
    fetch_modes.start()
    fetch_local.start()

    rows = jnp.concatenate([margin_rows[s:s + 1, :] for s in range(SUBS)], axis=1).astype(F32)
    source = jnp.floor((rows + 0.5) * (1.0 / HELD))
    within = rows - source * HELD
    place = lax.broadcasted_iota(jnp.int32, (OWNERS, OUTER), 0)
    owner = jnp.zeros((OWNERS, OUTER), jnp.int32)
    for j in range(OWNERS):
        owner = jnp.where(place == j, peers[j], owner)
    owned = source == owner.astype(F32)
    owned_b = jnp.where(owned, 1.0, 0.0).astype(BF16)

    def earlier(i, _):
        down = (lax.broadcasted_iota(jnp.int32, (STRIP, OUTER), 0) + i * STRIP).astype(F32)
        take[strip(i), :OUTER] = jnp.where(down < iota((STRIP, OUTER), 1), 1.0, 0.0).astype(BF16)
        return 0

    lax.fori_loop(0, OUTER // STRIP, earlier, 0)
    before = dot(owned_b, take[:, :OUTER])
    rank = jnp.sum(jnp.where(owned, before, 0.0), axis=0, keepdims=True)
    placed = jnp.sum(jnp.where(owned, before + CAP * place.astype(F32), 0.0), axis=0, keepdims=True)
    placed_row[...] = placed

    store_column(rank, picked.at[:OUTER])
    ranked = picked[:OUTER, :] == iota((OUTER, STRIP), 1)
    store_column(within + 1.0, picked.at[:OUTER])
    high, low = split_digits(jnp.where(ranked, picked[:OUTER, :], 0.0))
    ask = dot(owned_b, high) * 64.0 + dot(owned_b, low)
    asked[...] = jnp.broadcast_to(ask[:, None, :], (OWNERS, 8, STRIP))

    pl.semaphore_wait(barrier, jnp.where(stays, OWNERS - 1 + 3, OWNERS - 1 + 6))

    for j in range(SELF):
        pltpu.make_async_remote_copy(
            asked.at[j], wanted.at[BACK[j]], index_sem.at[0], index_sem.at[1],
            device_id=(peers[j], col), device_id_type=MESH,
        ).start()
    wanted[SELF] = asked[SELF]

    store_column(placed, picked.at[:OUTER])
    fill_by_column(take, picked)
    fill_by_row(take_t, placed_row)

    fetch_start.wait()

    def lower(s, _):
        pair[pl.ds(pl.multiple_of(s * CORE, CORE), CORE), :COLS] = x[pl.ds(pl.multiple_of(s * CORE, CORE), CORE), :].astype(BF16)
        return 0

    lax.fori_loop(0, SUBS, lower, 0)

    fetch_modes.wait()
    slot_modes_t[:, :OUTER] = jnp.zeros((COARSE, OUTER), BF16)
    for s in range(SUBS):
        slot_modes_t[s * MODES:(s + 1) * MODES, s * MARGIN:(s + 1) * MARGIN] = mt_v[s, :, CORE:]
    unit = jnp.where(iota((STRIP, STRIP), 0) == iota((STRIP, STRIP), 1), 1.0, 0.0).astype(BF16)
    for k in range(OUTER // STRIP):
        outer[k * STRIP:(k + 1) * STRIP, :] = lax.dot_general(
            unit, slot_modes_t[:, k * STRIP:(k + 1) * STRIP], (((1,), (1,)), ((), ())), preferred_element_type=F32
        ).astype(BF16)
    slot_modes[...] = dot(take_t[...], outer[...]).astype(BF16)
    slot_modes_t[...] = dot(slot_modes_t[:, :OUTER], take[...]).astype(BF16)

    for k in range(2):
        pltpu.make_async_copy(wanted.at[pl.ds(0, OWNERS - 1)], wanted.at[pl.ds(0, OWNERS - 1)], index_sem.at[k]).wait()
    slot_of = jnp.max(wanted[...], axis=1)
    high, low = split_digits(slot_of)
    slot = iota((STRIP, SLOTS), 1)
    owner_of = jnp.floor((slot + 0.5) * (1.0 / CAP))
    spread = jnp.where(slot - owner_of * CAP == iota((STRIP, SLOTS), 0), 1.0, 0.0).astype(BF16)
    wide = dot(high, spread) * 64.0 + dot(low, spread)
    row = jnp.sum(jnp.where(owner_of[:OWNERS] == iota((OWNERS, SLOTS), 0), wide, 0.0), axis=0, keepdims=True) - 1.0
    wanted_row[...] = row
    store_column(jnp.where(row < 0.0, -2.0, row), picked)
    fill_by_column(pick, picked)

    def ship(which):
        half = which % 2
        for j in range(SELF):
            pltpu.make_async_remote_copy(
                send.at[half, j], recv.at[which, BACK[j]], send_sem.at[which], recv_sem.at[which],
                device_id=(peers[j], col), device_id_type=MESH,
            ).start()
        recv[which, SELF] = send[half, SELF]

    def arrive(which):
        others = recv.at[which, pl.ds(0, OWNERS - 1)]
        pltpu.make_async_copy(others, others, recv_sem.at[which]).wait()
        pltpu.make_async_copy(others, others, send_sem.at[which]).wait()

    def tile(i):
        return pl.ds(pl.multiple_of(i * TILE, TILE), TILE)

    def put(which, i, value):
        send[which % 2, i * EACH:(i + 1) * EACH] = value.astype(BF16).reshape(EACH, CAP, COLS)

    def received(which):
        return recv[which].reshape(SLOTS, COLS)

    def rows_of(s):
        return pl.ds(pl.multiple_of(s * CORE, CORE), CORE)

    def margin_of(s):
        return pl.ds(pl.multiple_of(s * MARGIN, MARGIN), MARGIN)

    def halves(v):
        upper = v.astype(BF16)
        return upper, (v - upper.astype(F32)).astype(BF16)

    def joined(both):
        return both[:, :COLS] + both[:, COLS:]

    def pick_pairs():
        def split(s, _):
            pair[rows_of(s), :COLS], pair[rows_of(s), COLS:] = halves(base[rows_of(s), :])
            return 0

        lax.fori_loop(0, SUBS, split, 0)

        def body(i, _):
            picked[tile(i), :] = joined(dot(pick[tile(i), :], pair[...]))
            return 0

        lax.fori_loop(0, TILES, body, 0)

    def correct_picked(to, which, sign):
        arrived = received(which)
        for i in range(TILES):
            put(to, i, picked[i * TILE:(i + 1) * TILE, :] + sign * dot(same[i * TILE:(i + 1) * TILE, :], arrived))
        ship(to)

    for i in range(TILES):
        put(GATHER, i, dot(pick[i * TILE:(i + 1) * TILE, :], pair[:, :COLS]))
    ship(GATHER)

    pltpu.make_async_copy(base.at[:WIDTH], base.at[:WIDTH], bring.at[1]).wait()
    for k in range(WIDTH // STRIP):
        tile_t[k * STRIP:(k + 1) * STRIP, :] = base[k * STRIP:(k + 1) * STRIP, :].T.astype(BF16)

    def hand(end):
        pltpu.make_async_remote_copy(
            tile_t, block.at[at_y], coarse_sem.at[0], coarse_sem.at[1], device_id=end, device_id_type=MESH
        ).start()

    for d in range(1, ACROSS):
        hand(takers[d])

    @pl.when(stays)
    def _():
        block[at_y] = tile_t[...]

    @pl.when(jnp.logical_not(stays))
    def _():
        hand(takers[0])

    fill_equal(same, picked, wanted_row)
    fetch_stiff.wait()

    give_x = pltpu.make_async_copy(x, out_x, bring.at[6])

    def iteration(it, _):
        fetch_loads = pltpu.make_async_copy(loads, base, bring.at[5])
        fetch_loads.start()

        def from_core(s, _):
            loc[s, :CORE, :] = x[rows_of(s), :].astype(BF16)
            part[s] = dot(k_v[s, :, :CORE], loc[s, :CORE, :])
            return 0

        lax.fori_loop(0, SUBS, from_core, 0)

        @pl.when(it == ITERS)
        def _():
            give_x.start()

        arrive(GATHER)
        arrived = received(GATHER)
        for s in range(SUBS):
            near = slice(s * MARGIN, (s + 1) * MARGIN)
            margin = dot(take[near, :], arrived).astype(BF16)
            loc[s, CORE:, :] = margin
            outer[near, :] = (part[s, CORE:, :] + dot(k_v[s, CORE:, CORE:], margin)).astype(BF16)
        for i in range(TILES):
            put(SCATTER, i, dot(take_t[i * TILE:(i + 1) * TILE, :], outer[...]))
        ship(SCATTER)
        fetch_loads.wait()

        def core_part(s, _):
            base[rows_of(s), :] = base[rows_of(s), :] - (part[s, :CORE, :] + dot(k_v[s, :CORE, CORE:], loc[s, CORE:, :]))
            return 0

        lax.fori_loop(0, SUBS, core_part, 0)

        @pl.when(it < ITERS)
        def _():
            pick_pairs()

        arrive(SCATTER)

        @pl.when(it < ITERS)
        def _():
            correct_picked(REGATHER, SCATTER, -1.0)

        @pl.when(it == 0)
        def _():
            fill_by_row(pick_t, wanted_row)

        def finish_residual(s, _):
            base[rows_of(s), :] = base[rows_of(s), :] - dot(pick_t[rows_of(s), :], received(SCATTER))

            @pl.when(it == ITERS)
            def _():
                pltpu.make_async_copy(base.at[rows_of(s)], out_r.at[rows_of(s)], bring.at[7]).start()

            return 0

        lax.fori_loop(0, SUBS, finish_residual, 0)

        @pl.when(it < ITERS)
        def _():
            @pl.when(it == 0)
            def _():
                fetch_local.wait()
                for k in range(2):
                    @pl.when(stays)
                    def _():
                        pltpu.make_async_copy(block.at[:3], block.at[:3], coarse_sem.at[k]).wait()

                    @pl.when(jnp.logical_not(stays))
                    def _():
                        pltpu.make_async_copy(block, block, coarse_sem.at[k]).wait()

            def solve_core(s, _):
                loc[s, :CORE, :] = base[rows_of(s), :].astype(BF16)
                part[s] = dot(l_v[s, :, :CORE], loc[s, :CORE, :])
                return 0

            lax.fori_loop(0, SUBS, solve_core, 0)
            def finish_margin():
                def solve(s, _):
                    margin = dot(take[margin_of(s), :], received(REGATHER)).astype(BF16)
                    loc[s, CORE:, :] = margin
                    whole = part[s, CORE:, :] + dot(l_v[s, CORE:, CORE:], margin)
                    pair[margin_of(s), :COLS], pair[margin_of(s), COLS:] = halves(0.5 * whole)
                    return 0

                def in_slots(i, _):
                    picked[tile(i), :] = joined(dot(take_t[tile(i), :], pair[:OUTER, :]))
                    return 0

                lax.fori_loop(0, SUBS, solve, 0)
                lax.fori_loop(0, TILES, in_slots, 0)

            def finish_core():
                def solve(s, _):
                    whole = part[s, :CORE, :] + dot(l_v[s, :CORE, CORE:], loc[s, CORE:, :])
                    base[rows_of(s), :] = x[rows_of(s), :] + 0.5 * whole
                    return 0

                lax.fori_loop(0, SUBS, solve, 0)

            projected = jnp.concatenate([dot(mt_v[s, :, :CORE], loc[s, :CORE, :]) for s in range(SUBS)], axis=0)
            arrive(REGATHER)
            proj[pl.ds(at_y, 1)] = (projected + dot(slot_modes_t[...], received(REGATHER))).astype(BF16)[None]
            for dy in (2, 1, 3):
                pltpu.make_async_remote_copy(
                    proj.at[at_y], proj.at[at_y], proj_sem.at[0], proj_sem.at[1],
                    device_id=(lax.rem(at_y + dy, ROWS_Y) * PLANE + at_q, col), device_id_type=MESH,
                ).start()
            finish_margin()
            for k in range(2):
                pltpu.make_async_copy(proj.at[:3], proj.at[:3], proj_sem.at[k]).wait()
            total = dot(block[0], proj[0])
            for k in range(1, ROWS_Y):
                total = total + dot(block[k], proj[k])
            bits[...] = total.astype(BF16).reshape(PLANE, COARSE, COLS)
            for dz, dx in ((1, 2), (0, 2), (1, 1), (1, 3), (1, 0), (0, 1), (0, 3)):
                there = lax.rem(at_z + dz, 2) * 4 + lax.rem(at_x + dx, 4)
                pltpu.make_async_remote_copy(
                    bits.at[there], sums.at[at_q], sum_sem.at[0], sum_sem.at[1],
                    device_id=(at_y * PLANE + there, col), device_id_type=MESH,
                ).start()
            sums[pl.ds(at_q, 1)] = bits[pl.ds(at_q, 1)]
            finish_core()
            for k in range(2):
                pltpu.make_async_copy(sums.at[:PLANE - 1], sums.at[:PLANE - 1], sum_sem.at[k]).wait()
            coarse = sums[0].astype(F32)
            for k in range(1, PLANE):
                coarse = coarse + sums[k].astype(F32)
            coarse = jnp.concatenate(halves(coarse), axis=1)
            for i in range(TILES):
                lifted = joined(dot(slot_modes[i * TILE:(i + 1) * TILE, :], coarse))
                put(CORRECT, i, picked[i * TILE:(i + 1) * TILE, :] + lifted)
            ship(CORRECT)
            for s in range(SUBS):
                lifted = lax.dot_general(
                    mt_v[s, :, :CORE], coarse[s * MODES:(s + 1) * MODES], (((0,), (0,)), ((), ())),
                    preferred_element_type=F32,
                )
                base[s * CORE:(s + 1) * CORE, :] = base[s * CORE:(s + 1) * CORE, :] + joined(lifted)
            pick_pairs()
            arrive(CORRECT)
            correct_picked(GATHER, CORRECT, 1.0)

            def finish_step(s, _):
                x[rows_of(s), :] = base[rows_of(s), :] + dot(pick_t[rows_of(s), :], received(CORRECT))
                return 0

            lax.fori_loop(0, SUBS, finish_step, 0)

        return 0

    lax.fori_loop(0, ITERS + 1, iteration, 0)
    give_x.wait()
    pltpu.make_async_copy(base, out_r, bring.at[7]).wait()


def shards(loads, start, stiffness, local_inverse, modes, coarse_inverse, margin_rows):
    field = jax.ShapeDtypeStruct((HELD, COLS), F32)
    hbm = pl.BlockSpec(memory_space=pl.ANY)
    return pl.pallas_call(
        kernel,
        out_shape=(field, field),
        in_specs=[hbm] * 6 + [pl.BlockSpec(memory_space=pltpu.VMEM)],
        out_specs=(hbm, hbm),
        scratch_shapes=[
            pltpu.VMEM((SUBS, ORDER, ORDER), BF16),
            pltpu.VMEM((SUBS, ORDER, ORDER), BF16),
            pltpu.VMEM((SUBS, MODES, ORDER), BF16),
            pltpu.VMEM((WIDTH, COARSE), BF16),
            pltpu.VMEM((ROWS_Y, WIDTH, COARSE), BF16),
            pltpu.VMEM((HELD, COLS), F32),
            pltpu.VMEM((HELD, COLS), F32),
            pltpu.VMEM((HELD, 2 * COLS), BF16),
            pltpu.VMEM((SUBS, ORDER, COLS), BF16),
            pltpu.VMEM((SUBS, ORDER, COLS), F32),
            pltpu.VMEM((SLOTS, COLS), F32),
            pltpu.VMEM((SLOTS, HELD), BF16),
            pltpu.VMEM((HELD, SLOTS), BF16),
            pltpu.VMEM((SLOTS, SLOTS), BF16),
            pltpu.VMEM((OUTER, SLOTS), BF16),
            pltpu.VMEM((SLOTS, OUTER), BF16),
            pltpu.VMEM((SLOTS, COARSE), BF16),
            pltpu.VMEM((COARSE, SLOTS), BF16),
            pltpu.VMEM((1, OUTER), F32),
            pltpu.VMEM((1, SLOTS), F32),
            pltpu.VMEM((OUTER, COLS), BF16),
            pltpu.VMEM((OWNERS, 8, STRIP), F32),
            pltpu.VMEM((OWNERS, 8, STRIP), F32),
            pltpu.VMEM((2, OWNERS, CAP, COLS), BF16),
            pltpu.VMEM((4, OWNERS, CAP, COLS), BF16),
            pltpu.VMEM((ROWS_Y, COARSE, COLS), BF16),
            pltpu.VMEM((PLANE, COARSE, COLS), BF16),
            pltpu.VMEM((PLANE, COARSE, COLS), BF16),
            pltpu.SemaphoreType.DMA((8,)),
            pltpu.SemaphoreType.DMA((4,)),
            pltpu.SemaphoreType.DMA((4,)),
            pltpu.SemaphoreType.DMA((2,)),
            pltpu.SemaphoreType.DMA((2,)),
            pltpu.SemaphoreType.DMA((2,)),
            pltpu.SemaphoreType.DMA((2,)),
        ],
        compiler_params=pltpu.CompilerParams(
            collective_id=0, has_side_effects=True, vmem_limit_bytes=63 * 1024 * 1024
        ),
    )(loads, start, stiffness, local_inverse, jnp.swapaxes(modes, 1, 2), coarse_inverse, margin_rows)


def solution(mesh):
    placed = (
        P("wide", "narrow"),
        P("wide", "narrow"),
        P("wide", None, None),
        P("wide", None, None),
        P("wide", None, None),
        P("wide", "narrow"),
        P("wide", None),
    )
    return jax.shard_map(
        shards,
        mesh=mesh,
        in_specs=placed,
        out_specs=(P("wide", "narrow"), P("wide", "narrow")),
        check_vma=False,
    )
```

```python
import jax
import jax.numpy as jnp
from jax import lax
from jax.experimental import pallas as pl
from jax.experimental.pallas import tpu as pltpu
from jax.sharding import PartitionSpec as P

MESH = pl.DeviceIdType.MESH
ITERS = 2
SUBS = 4
ORDER = 1024
TILE = 384
CORE = 768
MARGIN = ORDER - CORE
COLS = 128
MODES = 32
HELD = SUBS * CORE
OUTER = SUBS * MARGIN
OWNERS = 32
ACROSS = 4
CAP = 48
SLOTS = OWNERS * CAP
TILES = SLOTS // TILE
EACH = TILE // CAP
COARSE = SUBS * MODES
WIDTH = 1024
STRIP = 128
ROWS_Y = 4
PLANE = 8
F32 = jnp.float32
BF16 = jnp.bfloat16
GATHER, SCATTER, REGATHER, CORRECT = 0, 1, 2, 3
SIDES = (4, 2, 4)


def reach(offset):
    return sum(min(o, n - o) for o, n in zip(offset, SIDES))


OFFSETS = sorted(
    [(dy, dz, dx) for dy in range(SIDES[0]) for dz in range(SIDES[1]) for dx in range(SIDES[2])],
    key=reach, reverse=True,
)
BACK = [OFFSETS.index(tuple((n - o) % n for o, n in zip(offset, SIDES))) for offset in OFFSETS]
SELF = OWNERS - 1


def dot(a, b):
    return jnp.dot(a, b, preferred_element_type=F32)


def iota(shape, axis):
    return lax.broadcasted_iota(jnp.int32, shape, axis).astype(F32)


def strip(i):
    return pl.ds(pl.multiple_of(i * STRIP, STRIP), STRIP)


def split_digits(v):
    high = jnp.floor(v * (1.0 / 64.0))
    return high.astype(BF16), (v - high * 64.0).astype(BF16)


def store_column(row, ref):
    same = iota((STRIP, STRIP), 0) == iota((STRIP, STRIP), 1)
    for k in range(row.shape[1] // STRIP):
        piece = jnp.broadcast_to(row[:, k * STRIP:(k + 1) * STRIP], (STRIP, STRIP))
        column = jnp.sum(jnp.where(same, piece, 0.0), axis=1, keepdims=True)
        ref[k * STRIP:(k + 1) * STRIP, :] = jnp.broadcast_to(column, (STRIP, STRIP))


def fill_by_column(out, column):
    rows, width = out.shape

    def body(i, _):
        held = column[strip(i), :]
        lanes = iota((STRIP, STRIP), 1)
        for k in range(width // STRIP):
            out[strip(i), k * STRIP:(k + 1) * STRIP] = jnp.where(held == lanes + float(k * STRIP), 1.0, 0.0).astype(BF16)
        return 0

    lax.fori_loop(0, rows // STRIP, body, 0)


def fill_by_row(out, row):
    rows, width = out.shape

    def body(i, _):
        down = (lax.broadcasted_iota(jnp.int32, (STRIP, STRIP), 0) + i * STRIP).astype(F32)
        for k in range(width // STRIP):
            out[strip(i), k * STRIP:(k + 1) * STRIP] = jnp.where(down == row[:, k * STRIP:(k + 1) * STRIP], 1.0, 0.0).astype(BF16)
        return 0

    lax.fori_loop(0, rows // STRIP, body, 0)


def fill_equal(out, column, row):
    rows, width = out.shape

    def body(i, _):
        held = column[strip(i), :]
        for k in range(width // STRIP):
            out[strip(i), k * STRIP:(k + 1) * STRIP] = jnp.where(held == row[:, k * STRIP:(k + 1) * STRIP], 1.0, 0.0).astype(BF16)
        return 0

    lax.fori_loop(0, rows // STRIP, body, 0)


def kernel(
    loads, start, stiffness, local_inverse, modes_t, coarse_inverse, margin_rows,
    out_x, out_r,
    k_v, l_v, mt_v, tile_t, block, x, base, pair, loc, part, picked,
    pick, pick_t, same, take, take_t, slot_modes, slot_modes_t, placed_row, wanted_row,
    outer, asked, wanted, send, recv, proj, bits, sums, bring, recv_sem, send_sem, index_sem, proj_sem, sum_sem, tile_sem, coarse_sem,
):
    me = lax.axis_index("wide")
    col = lax.axis_index("narrow")
    at_y, at_z, at_x = me // 8, lax.rem(me // 4, 2), lax.rem(me, 4)
    peers = [
        (lax.rem(at_y + dy, 4) * 2 + lax.rem(at_z + dz, 2)) * 4 + lax.rem(at_x + dx, 4) for dy, dz, dx in OFFSETS
    ]
    barrier = pltpu.get_barrier_semaphore()
    for j in range(SELF):
        pl.semaphore_signal(barrier, inc=1, device_id=(peers[j], col), device_id_type=MESH)
    for d in range(1, ACROSS):
        pl.semaphore_signal(barrier, inc=1, device_id=(me, lax.rem(col + d, ACROSS)), device_id_type=MESH)

    at_q = lax.rem(me, PLANE)
    stays = col == at_y
    partner = (col * PLANE + at_q, at_y)

    @pl.when(jnp.logical_not(stays))
    def _():
        pl.semaphore_signal(barrier, inc=1, device_id=partner, device_id_type=MESH)

    fetch_start = pltpu.make_async_copy(start, x, bring.at[0])
    fetch_stiff = pltpu.make_async_copy(stiffness, k_v, bring.at[2])
    fetch_modes = pltpu.make_async_copy(modes_t, mt_v, bring.at[3])
    fetch_local = pltpu.make_async_copy(local_inverse, l_v, bring.at[4])
    fetch_start.start()
    for k in range(WIDTH // STRIP):
        pltpu.make_async_copy(
            coarse_inverse.at[:, k * STRIP:(k + 1) * STRIP], base.at[k * STRIP:(k + 1) * STRIP], bring.at[1]
        ).start()
    fetch_stiff.start()
    fetch_modes.start()
    fetch_local.start()

    rows = jnp.concatenate([margin_rows[s:s + 1, :] for s in range(SUBS)], axis=1).astype(F32)
    source = jnp.floor((rows + 0.5) * (1.0 / HELD))
    within = rows - source * HELD
    place = lax.broadcasted_iota(jnp.int32, (OWNERS, OUTER), 0)
    owner = jnp.zeros((OWNERS, OUTER), jnp.int32)
    for j in range(OWNERS):
        owner = jnp.where(place == j, peers[j], owner)
    owned = source == owner.astype(F32)
    owned_b = jnp.where(owned, 1.0, 0.0).astype(BF16)

    def earlier(i, _):
        down = (lax.broadcasted_iota(jnp.int32, (STRIP, OUTER), 0) + i * STRIP).astype(F32)
        take[strip(i), :OUTER] = jnp.where(down < iota((STRIP, OUTER), 1), 1.0, 0.0).astype(BF16)
        return 0

    lax.fori_loop(0, OUTER // STRIP, earlier, 0)
    before = dot(owned_b, take[:, :OUTER])
    rank = jnp.sum(jnp.where(owned, before, 0.0), axis=0, keepdims=True)
    placed = jnp.sum(jnp.where(owned, before + CAP * place.astype(F32), 0.0), axis=0, keepdims=True)
    placed_row[...] = placed

    store_column(rank, picked.at[:OUTER])
    ranked = picked[:OUTER, :] == iota((OUTER, STRIP), 1)
    store_column(within + 1.0, picked.at[:OUTER])
    high, low = split_digits(jnp.where(ranked, picked[:OUTER, :], 0.0))
    ask = dot(owned_b, high) * 64.0 + dot(owned_b, low)
    asked[...] = jnp.broadcast_to(ask[:, None, :], (OWNERS, 8, STRIP))

    pltpu.make_async_copy(base.at[:WIDTH], base.at[:WIDTH], bring.at[1]).wait()
    for k in range(WIDTH // STRIP):
        tile_t[k * STRIP:(k + 1) * STRIP, :] = base[k * STRIP:(k + 1) * STRIP, :].T.astype(BF16)

    pl.semaphore_wait(barrier, jnp.where(stays, OWNERS - 1 + 3, OWNERS - 1 + 4))

    for j in range(SELF):
        pltpu.make_async_remote_copy(
            asked.at[j], wanted.at[BACK[j]], index_sem.at[0], index_sem.at[1],
            device_id=(peers[j], col), device_id_type=MESH,
        ).start()
    wanted[SELF] = asked[SELF]

    @pl.when(stays)
    def _():
        block[col] = tile_t[...]

    @pl.when(jnp.logical_not(stays))
    def _():
        pltpu.make_async_remote_copy(
            tile_t, block.at[at_y], tile_sem.at[0], tile_sem.at[1], device_id=partner, device_id_type=MESH
        ).start()

    store_column(placed, picked.at[:OUTER])
    fill_by_column(take, picked)
    fill_by_row(take_t, placed_row)

    fetch_start.wait()

    def lower(s, _):
        pair[pl.ds(pl.multiple_of(s * CORE, CORE), CORE), :COLS] = x[pl.ds(pl.multiple_of(s * CORE, CORE), CORE), :].astype(BF16)
        return 0

    lax.fori_loop(0, SUBS, lower, 0)

    fetch_modes.wait()
    slot_modes_t[:, :OUTER] = jnp.zeros((COARSE, OUTER), BF16)
    for s in range(SUBS):
        slot_modes_t[s * MODES:(s + 1) * MODES, s * MARGIN:(s + 1) * MARGIN] = mt_v[s, :, CORE:]
    unit = jnp.where(iota((STRIP, STRIP), 0) == iota((STRIP, STRIP), 1), 1.0, 0.0).astype(BF16)
    for k in range(OUTER // STRIP):
        outer[k * STRIP:(k + 1) * STRIP, :] = lax.dot_general(
            unit, slot_modes_t[:, k * STRIP:(k + 1) * STRIP], (((1,), (1,)), ((), ())), preferred_element_type=F32
        ).astype(BF16)
    slot_modes[...] = dot(take_t[...], outer[...]).astype(BF16)
    slot_modes_t[...] = dot(slot_modes_t[:, :OUTER], take[...]).astype(BF16)

    for k in range(2):
        pltpu.make_async_copy(wanted.at[pl.ds(0, OWNERS - 1)], wanted.at[pl.ds(0, OWNERS - 1)], index_sem.at[k]).wait()
    slot_of = jnp.max(wanted[...], axis=1)
    high, low = split_digits(slot_of)
    slot = iota((STRIP, SLOTS), 1)
    owner_of = jnp.floor((slot + 0.5) * (1.0 / CAP))
    spread = jnp.where(slot - owner_of * CAP == iota((STRIP, SLOTS), 0), 1.0, 0.0).astype(BF16)
    wide = dot(high, spread) * 64.0 + dot(low, spread)
    row = jnp.sum(jnp.where(owner_of[:OWNERS] == iota((OWNERS, SLOTS), 0), wide, 0.0), axis=0, keepdims=True) - 1.0
    wanted_row[...] = row
    store_column(jnp.where(row < 0.0, -2.0, row), picked)
    fill_by_column(pick, picked)

    def ship(which):
        half = which % 2
        for j in range(SELF):
            pltpu.make_async_remote_copy(
                send.at[half, j], recv.at[which, BACK[j]], send_sem.at[which], recv_sem.at[which],
                device_id=(peers[j], col), device_id_type=MESH,
            ).start()
        recv[which, SELF] = send[half, SELF]

    def arrive(which):
        others = recv.at[which, pl.ds(0, OWNERS - 1)]
        pltpu.make_async_copy(others, others, recv_sem.at[which]).wait()
        pltpu.make_async_copy(others, others, send_sem.at[which]).wait()

    def tile(i):
        return pl.ds(pl.multiple_of(i * TILE, TILE), TILE)

    def put(which, i, value):
        send[which % 2, i * EACH:(i + 1) * EACH] = value.astype(BF16).reshape(EACH, CAP, COLS)

    def received(which):
        return recv[which].reshape(SLOTS, COLS)

    def rows_of(s):
        return pl.ds(pl.multiple_of(s * CORE, CORE), CORE)

    def margin_of(s):
        return pl.ds(pl.multiple_of(s * MARGIN, MARGIN), MARGIN)

    def halves(v):
        upper = v.astype(BF16)
        return upper, (v - upper.astype(F32)).astype(BF16)

    def joined(both):
        return both[:, :COLS] + both[:, COLS:]

    def pick_pairs():
        def split(s, _):
            pair[rows_of(s), :COLS], pair[rows_of(s), COLS:] = halves(base[rows_of(s), :])
            return 0

        lax.fori_loop(0, SUBS, split, 0)

        def body(i, _):
            picked[tile(i), :] = joined(dot(pick[tile(i), :], pair[...]))
            return 0

        lax.fori_loop(0, TILES, body, 0)

    def correct_picked(to, which, sign):
        arrived = received(which)
        for i in range(TILES):
            put(to, i, picked[i * TILE:(i + 1) * TILE, :] + sign * dot(same[i * TILE:(i + 1) * TILE, :], arrived))
        ship(to)

    for i in range(TILES):
        put(GATHER, i, dot(pick[i * TILE:(i + 1) * TILE, :], pair[:, :COLS]))
    ship(GATHER)

    @pl.when(jnp.logical_not(stays))
    def _():
        for k in range(2):
            pltpu.make_async_copy(tile_t, tile_t, tile_sem.at[k]).wait()

    for d in range(1, ACROSS):
        pltpu.make_async_remote_copy(
            block.at[col], block.at[col], coarse_sem.at[0], coarse_sem.at[1],
            device_id=(me, lax.rem(col + d, ACROSS)), device_id_type=MESH,
        ).start()

    fill_equal(same, picked, wanted_row)
    fetch_stiff.wait()

    give_x = pltpu.make_async_copy(x, out_x, bring.at[6])

    def iteration(it, _):
        fetch_loads = pltpu.make_async_copy(loads, base, bring.at[5])
        fetch_loads.start()

        def from_core(s, _):
            loc[s, :CORE, :] = x[rows_of(s), :].astype(BF16)
            part[s] = dot(k_v[s, :, :CORE], loc[s, :CORE, :])
            return 0

        lax.fori_loop(0, SUBS, from_core, 0)

        @pl.when(it == ITERS)
        def _():
            give_x.start()

        arrive(GATHER)
        arrived = received(GATHER)
        for s in range(SUBS):
            near = slice(s * MARGIN, (s + 1) * MARGIN)
            margin = dot(take[near, :], arrived).astype(BF16)
            loc[s, CORE:, :] = margin
            outer[near, :] = (part[s, CORE:, :] + dot(k_v[s, CORE:, CORE:], margin)).astype(BF16)
        for i in range(TILES):
            put(SCATTER, i, dot(take_t[i * TILE:(i + 1) * TILE, :], outer[...]))
        ship(SCATTER)
        fetch_loads.wait()

        def core_part(s, _):
            base[rows_of(s), :] = base[rows_of(s), :] - (part[s, :CORE, :] + dot(k_v[s, :CORE, CORE:], loc[s, CORE:, :]))
            return 0

        lax.fori_loop(0, SUBS, core_part, 0)

        @pl.when(it < ITERS)
        def _():
            pick_pairs()

        arrive(SCATTER)

        @pl.when(it < ITERS)
        def _():
            correct_picked(REGATHER, SCATTER, -1.0)

        @pl.when(it == 0)
        def _():
            fill_by_row(pick_t, wanted_row)

        def finish_residual(s, _):
            base[rows_of(s), :] = base[rows_of(s), :] - dot(pick_t[rows_of(s), :], received(SCATTER))

            @pl.when(it == ITERS)
            def _():
                pltpu.make_async_copy(base.at[rows_of(s)], out_r.at[rows_of(s)], bring.at[7]).start()

            return 0

        lax.fori_loop(0, SUBS, finish_residual, 0)

        @pl.when(it < ITERS)
        def _():
            @pl.when(it == 0)
            def _():
                fetch_local.wait()
                for k in range(2):
                    pltpu.make_async_copy(block.at[:3], block.at[:3], coarse_sem.at[k]).wait()

            def solve_core(s, _):
                loc[s, :CORE, :] = base[rows_of(s), :].astype(BF16)
                part[s] = dot(l_v[s, :, :CORE], loc[s, :CORE, :])
                return 0

            lax.fori_loop(0, SUBS, solve_core, 0)
            def finish_margin():
                def solve(s, _):
                    margin = dot(take[margin_of(s), :], received(REGATHER)).astype(BF16)
                    loc[s, CORE:, :] = margin
                    whole = part[s, CORE:, :] + dot(l_v[s, CORE:, CORE:], margin)
                    pair[margin_of(s), :COLS], pair[margin_of(s), COLS:] = halves(0.5 * whole)
                    return 0

                def in_slots(i, _):
                    picked[tile(i), :] = joined(dot(take_t[tile(i), :], pair[:OUTER, :]))
                    return 0

                lax.fori_loop(0, SUBS, solve, 0)
                lax.fori_loop(0, TILES, in_slots, 0)

            def finish_core():
                def solve(s, _):
                    whole = part[s, :CORE, :] + dot(l_v[s, :CORE, CORE:], loc[s, CORE:, :])
                    base[rows_of(s), :] = x[rows_of(s), :] + 0.5 * whole
                    return 0

                lax.fori_loop(0, SUBS, solve, 0)

            projected = jnp.concatenate([dot(mt_v[s, :, :CORE], loc[s, :CORE, :]) for s in range(SUBS)], axis=0)
            arrive(REGATHER)
            proj[pl.ds(at_y, 1)] = (projected + dot(slot_modes_t[...], received(REGATHER))).astype(BF16)[None]
            for dy in (2, 1, 3):
                pltpu.make_async_remote_copy(
                    proj.at[at_y], proj.at[at_y], proj_sem.at[0], proj_sem.at[1],
                    device_id=(lax.rem(at_y + dy, ROWS_Y) * PLANE + at_q, col), device_id_type=MESH,
                ).start()
            finish_margin()
            for k in range(2):
                pltpu.make_async_copy(proj.at[:3], proj.at[:3], proj_sem.at[k]).wait()
            total = dot(block[0], proj[0])
            for k in range(1, ROWS_Y):
                total = total + dot(block[k], proj[k])
            bits[...] = total.astype(BF16).reshape(PLANE, COARSE, COLS)
            for dz, dx in ((1, 2), (0, 2), (1, 1), (1, 3), (1, 0), (0, 1), (0, 3)):
                there = lax.rem(at_z + dz, 2) * 4 + lax.rem(at_x + dx, 4)
                pltpu.make_async_remote_copy(
                    bits.at[there], sums.at[at_q], sum_sem.at[0], sum_sem.at[1],
                    device_id=(at_y * PLANE + there, col), device_id_type=MESH,
                ).start()
            sums[pl.ds(at_q, 1)] = bits[pl.ds(at_q, 1)]
            finish_core()
            for k in range(2):
                pltpu.make_async_copy(sums.at[:PLANE - 1], sums.at[:PLANE - 1], sum_sem.at[k]).wait()
            coarse = sums[0].astype(F32)
            for k in range(1, PLANE):
                coarse = coarse + sums[k].astype(F32)
            coarse = jnp.concatenate(halves(coarse), axis=1)
            for i in range(TILES):
                lifted = joined(dot(slot_modes[i * TILE:(i + 1) * TILE, :], coarse))
                put(CORRECT, i, picked[i * TILE:(i + 1) * TILE, :] + lifted)
            ship(CORRECT)
            for s in range(SUBS):
                lifted = lax.dot_general(
                    mt_v[s, :, :CORE], coarse[s * MODES:(s + 1) * MODES], (((0,), (0,)), ((), ())),
                    preferred_element_type=F32,
                )
                base[s * CORE:(s + 1) * CORE, :] = base[s * CORE:(s + 1) * CORE, :] + joined(lifted)
            pick_pairs()
            arrive(CORRECT)
            correct_picked(GATHER, CORRECT, 1.0)

            def finish_step(s, _):
                x[rows_of(s), :] = base[rows_of(s), :] + dot(pick_t[rows_of(s), :], received(CORRECT))
                return 0

            lax.fori_loop(0, SUBS, finish_step, 0)

        return 0

    lax.fori_loop(0, ITERS + 1, iteration, 0)
    give_x.wait()
    pltpu.make_async_copy(base, out_r, bring.at[7]).wait()


def shards(loads, start, stiffness, local_inverse, modes, coarse_inverse, margin_rows):
    field = jax.ShapeDtypeStruct((HELD, COLS), F32)
    hbm = pl.BlockSpec(memory_space=pl.ANY)
    return pl.pallas_call(
        kernel,
        out_shape=(field, field),
        in_specs=[hbm] * 6 + [pl.BlockSpec(memory_space=pltpu.VMEM)],
        out_specs=(hbm, hbm),
        scratch_shapes=[
            pltpu.VMEM((SUBS, ORDER, ORDER), BF16),
            pltpu.VMEM((SUBS, ORDER, ORDER), BF16),
            pltpu.VMEM((SUBS, MODES, ORDER), BF16),
            pltpu.VMEM((WIDTH, COARSE), BF16),
            pltpu.VMEM((ROWS_Y, WIDTH, COARSE), BF16),
            pltpu.VMEM((HELD, COLS), F32),
            pltpu.VMEM((HELD, COLS), F32),
            pltpu.VMEM((HELD, 2 * COLS), BF16),
            pltpu.VMEM((SUBS, ORDER, COLS), BF16),
            pltpu.VMEM((SUBS, ORDER, COLS), F32),
            pltpu.VMEM((SLOTS, COLS), F32),
            pltpu.VMEM((SLOTS, HELD), BF16),
            pltpu.VMEM((HELD, SLOTS), BF16),
            pltpu.VMEM((SLOTS, SLOTS), BF16),
            pltpu.VMEM((OUTER, SLOTS), BF16),
            pltpu.VMEM((SLOTS, OUTER), BF16),
            pltpu.VMEM((SLOTS, COARSE), BF16),
            pltpu.VMEM((COARSE, SLOTS), BF16),
            pltpu.VMEM((1, OUTER), F32),
            pltpu.VMEM((1, SLOTS), F32),
            pltpu.VMEM((OUTER, COLS), BF16),
            pltpu.VMEM((OWNERS, 8, STRIP), F32),
            pltpu.VMEM((OWNERS, 8, STRIP), F32),
            pltpu.VMEM((2, OWNERS, CAP, COLS), BF16),
            pltpu.VMEM((4, OWNERS, CAP, COLS), BF16),
            pltpu.VMEM((ROWS_Y, COARSE, COLS), BF16),
            pltpu.VMEM((PLANE, COARSE, COLS), BF16),
            pltpu.VMEM((PLANE, COARSE, COLS), BF16),
            pltpu.SemaphoreType.DMA((8,)),
            pltpu.SemaphoreType.DMA((4,)),
            pltpu.SemaphoreType.DMA((4,)),
            pltpu.SemaphoreType.DMA((2,)),
            pltpu.SemaphoreType.DMA((2,)),
            pltpu.SemaphoreType.DMA((2,)),
            pltpu.SemaphoreType.DMA((2,)),
            pltpu.SemaphoreType.DMA((2,)),
        ],
        compiler_params=pltpu.CompilerParams(
            collective_id=0, has_side_effects=True, vmem_limit_bytes=63 * 1024 * 1024
        ),
    )(loads, start, stiffness, local_inverse, jnp.swapaxes(modes, 1, 2), coarse_inverse, margin_rows)


def solution(mesh):
    placed = (
        P("wide", "narrow"),
        P("wide", "narrow"),
        P("wide", None, None),
        P("wide", None, None),
        P("wide", None, None),
        P("wide", "narrow"),
        P("wide", None),
    )
    return jax.shard_map(
        shards,
        mesh=mesh,
        in_specs=placed,
        out_specs=(P("wide", "narrow"), P("wide", "narrow")),
        check_vma=False,
    )
```

```python
import jax
import jax.numpy as jnp
from jax import lax
from jax.experimental import pallas as pl
from jax.experimental.pallas import tpu as pltpu
from jax.sharding import PartitionSpec as P

MESH = pl.DeviceIdType.MESH
ITERS = 2
SUBS = 4
ORDER = 1024
TILE = 768
CORE = 768
MARGIN = ORDER - CORE
COLS = 128
MODES = 32
HELD = SUBS * CORE
OUTER = SUBS * MARGIN
OWNERS = 32
ACROSS = 4
CAP = 48
SLOTS = OWNERS * CAP
TILES = SLOTS // TILE
EACH = TILE // CAP
COARSE = SUBS * MODES
WIDTH = 1024
STRIP = 128
ROWS_Y = 4
PLANE = 8
F32 = jnp.float32
BF16 = jnp.bfloat16
GATHER, SCATTER, REGATHER, CORRECT = 0, 1, 2, 3
SIDES = (4, 2, 4)


def reach(offset):
    return sum(min(o, n - o) for o, n in zip(offset, SIDES))


OFFSETS = sorted(
    [(dy, dz, dx) for dy in range(SIDES[0]) for dz in range(SIDES[1]) for dx in range(SIDES[2])],
    key=reach, reverse=True,
)
BACK = [OFFSETS.index(tuple((n - o) % n for o, n in zip(offset, SIDES))) for offset in OFFSETS]
SELF = OWNERS - 1


def dot(a, b):
    return jnp.dot(a, b, preferred_element_type=F32)


def iota(shape, axis):
    return lax.broadcasted_iota(jnp.int32, shape, axis).astype(F32)


def strip(i):
    return pl.ds(pl.multiple_of(i * STRIP, STRIP), STRIP)


def split_digits(v):
    high = jnp.floor(v * (1.0 / 64.0))
    return high.astype(BF16), (v - high * 64.0).astype(BF16)


def store_column(row, ref):
    same = iota((STRIP, STRIP), 0) == iota((STRIP, STRIP), 1)
    for k in range(row.shape[1] // STRIP):
        piece = jnp.broadcast_to(row[:, k * STRIP:(k + 1) * STRIP], (STRIP, STRIP))
        column = jnp.sum(jnp.where(same, piece, 0.0), axis=1, keepdims=True)
        ref[k * STRIP:(k + 1) * STRIP, :] = jnp.broadcast_to(column, (STRIP, STRIP))


def fill_by_column(out, column):
    rows, width = out.shape

    def body(i, _):
        held = column[strip(i), :]
        piece = jnp.floor(held * (1.0 / STRIP))
        lane = jnp.where(held - piece * STRIP == iota((STRIP, STRIP), 1), 1.0, 0.0).astype(BF16)
        piece = piece.astype(BF16)
        nothing = jnp.zeros((STRIP, STRIP), BF16)
        for k in range(width // STRIP):
            out[strip(i), k * STRIP:(k + 1) * STRIP] = jnp.where(piece == jnp.asarray(k, BF16), lane, nothing)
        return 0

    lax.fori_loop(0, rows // STRIP, body, 0)


def fill_by_row(out, row):
    rows, width = out.shape

    def body(i, _):
        down = (lax.broadcasted_iota(jnp.int32, (STRIP, STRIP), 0) + i * STRIP).astype(F32)
        for k in range(width // STRIP):
            out[strip(i), k * STRIP:(k + 1) * STRIP] = jnp.where(down == row[:, k * STRIP:(k + 1) * STRIP], 1.0, 0.0).astype(BF16)
        return 0

    lax.fori_loop(0, rows // STRIP, body, 0)


def fill_equal(out, column, row):
    rows, width = out.shape

    def body(i, _):
        held = column[strip(i), :]
        for k in range(width // STRIP):
            out[strip(i), k * STRIP:(k + 1) * STRIP] = jnp.where(held == row[:, k * STRIP:(k + 1) * STRIP], 1.0, 0.0).astype(BF16)
        return 0

    lax.fori_loop(0, rows // STRIP, body, 0)


def kernel(
    loads, start, stiffness, local_inverse, modes_t, coarse_inverse, margin_rows,
    out_x, out_r,
    k_v, l_v, mt_v, tile_t, block, x, base, pair, loc, part, picked,
    pick, pick_t, same, take, take_t, slot_modes, slot_modes_t, placed_row, wanted_row,
    outer, asked, wanted, send, recv, proj, bits, sums, bring, recv_sem, send_sem, index_sem, proj_sem, sum_sem, tile_sem, coarse_sem,
):
    me = lax.axis_index("wide")
    col = lax.axis_index("narrow")
    at_y, at_z, at_x = me // 8, lax.rem(me // 4, 2), lax.rem(me, 4)
    peers = [
        (lax.rem(at_y + dy, 4) * 2 + lax.rem(at_z + dz, 2)) * 4 + lax.rem(at_x + dx, 4) for dy, dz, dx in OFFSETS
    ]
    barrier = pltpu.get_barrier_semaphore()
    for j in range(SELF):
        pl.semaphore_signal(barrier, inc=1, device_id=(peers[j], col), device_id_type=MESH)
    for d in range(1, ACROSS):
        pl.semaphore_signal(barrier, inc=1, device_id=(me, lax.rem(col + d, ACROSS)), device_id_type=MESH)

    at_q = lax.rem(me, PLANE)
    stays = col == at_y
    partner = (col * PLANE + at_q, at_y)

    @pl.when(jnp.logical_not(stays))
    def _():
        pl.semaphore_signal(barrier, inc=1, device_id=partner, device_id_type=MESH)

    fetch_start = pltpu.make_async_copy(start, x, bring.at[0])
    fetch_stiff = pltpu.make_async_copy(stiffness, k_v, bring.at[2])
    fetch_modes = pltpu.make_async_copy(modes_t, mt_v, bring.at[3])
    fetch_local = pltpu.make_async_copy(local_inverse, l_v, bring.at[4])
    fetch_start.start()
    for k in range(WIDTH // STRIP):
        pltpu.make_async_copy(
            coarse_inverse.at[:, k * STRIP:(k + 1) * STRIP], base.at[k * STRIP:(k + 1) * STRIP], bring.at[1]
        ).start()
    fetch_stiff.start()
    fetch_modes.start()
    fetch_local.start()

    rows = jnp.concatenate([margin_rows[s:s + 1, :] for s in range(SUBS)], axis=1).astype(F32)
    source = jnp.floor((rows + 0.5) * (1.0 / HELD))
    within = rows - source * HELD
    place = lax.broadcasted_iota(jnp.int32, (OWNERS, OUTER), 0)
    owner = jnp.zeros((OWNERS, OUTER), jnp.int32)
    for j in range(OWNERS):
        owner = jnp.where(place == j, peers[j], owner)
    owned = source == owner.astype(F32)
    owned_b = jnp.where(owned, 1.0, 0.0).astype(BF16)

    def earlier(i, _):
        down = (lax.broadcasted_iota(jnp.int32, (STRIP, OUTER), 0) + i * STRIP).astype(F32)
        take[strip(i), :OUTER] = jnp.where(down < iota((STRIP, OUTER), 1), 1.0, 0.0).astype(BF16)
        return 0

    lax.fori_loop(0, OUTER // STRIP, earlier, 0)
    before = dot(owned_b, take[:, :OUTER])
    rank = jnp.sum(jnp.where(owned, before, 0.0), axis=0, keepdims=True)
    placed = jnp.sum(jnp.where(owned, before + CAP * place.astype(F32), 0.0), axis=0, keepdims=True)
    placed_row[...] = placed

    store_column(rank, picked.at[:OUTER])
    ranked = picked[:OUTER, :] == iota((OUTER, STRIP), 1)
    store_column(within + 1.0, picked.at[:OUTER])
    high, low = split_digits(jnp.where(ranked, picked[:OUTER, :], 0.0))
    ask = dot(owned_b, high) * 64.0 + dot(owned_b, low)
    asked[...] = jnp.broadcast_to(ask[:, None, :], (OWNERS, 8, STRIP))

    pltpu.make_async_copy(base.at[:WIDTH], base.at[:WIDTH], bring.at[1]).wait()
    for k in range(WIDTH // STRIP):
        tile_t[k * STRIP:(k + 1) * STRIP, :] = base[k * STRIP:(k + 1) * STRIP, :].T.astype(BF16)

    pl.semaphore_wait(barrier, jnp.where(stays, OWNERS - 1 + 3, OWNERS - 1 + 4))

    for j in range(SELF):
        pltpu.make_async_remote_copy(
            asked.at[j], wanted.at[BACK[j]], index_sem.at[0], index_sem.at[1],
            device_id=(peers[j], col), device_id_type=MESH,
        ).start()
    wanted[SELF] = asked[SELF]

    @pl.when(stays)
    def _():
        block[col] = tile_t[...]

    @pl.when(jnp.logical_not(stays))
    def _():
        pltpu.make_async_remote_copy(
            tile_t, block.at[at_y], tile_sem.at[0], tile_sem.at[1], device_id=partner, device_id_type=MESH
        ).start()

    store_column(placed, picked.at[:OUTER])
    fill_by_column(take, picked)
    fill_by_row(take_t, placed_row)

    fetch_start.wait()

    def lower(s, _):
        pair[pl.ds(pl.multiple_of(s * CORE, CORE), CORE), :COLS] = x[pl.ds(pl.multiple_of(s * CORE, CORE), CORE), :].astype(BF16)
        return 0

    lax.fori_loop(0, SUBS, lower, 0)

    fetch_modes.wait()
    slot_modes_t[:, :OUTER] = jnp.zeros((COARSE, OUTER), BF16)
    for s in range(SUBS):
        slot_modes_t[s * MODES:(s + 1) * MODES, s * MARGIN:(s + 1) * MARGIN] = mt_v[s, :, CORE:]
    unit = jnp.where(iota((STRIP, STRIP), 0) == iota((STRIP, STRIP), 1), 1.0, 0.0).astype(BF16)
    for k in range(OUTER // STRIP):
        outer[k * STRIP:(k + 1) * STRIP, :] = lax.dot_general(
            unit, slot_modes_t[:, k * STRIP:(k + 1) * STRIP], (((1,), (1,)), ((), ())), preferred_element_type=F32
        ).astype(BF16)
    slot_modes[...] = dot(take_t[...], outer[...]).astype(BF16)
    slot_modes_t[...] = dot(slot_modes_t[:, :OUTER], take[...]).astype(BF16)

    for k in range(2):
        pltpu.make_async_copy(wanted.at[pl.ds(0, OWNERS - 1)], wanted.at[pl.ds(0, OWNERS - 1)], index_sem.at[k]).wait()
    slot_of = jnp.max(wanted[...], axis=1)
    high, low = split_digits(slot_of)
    slot = iota((STRIP, SLOTS), 1)
    owner_of = jnp.floor((slot + 0.5) * (1.0 / CAP))
    spread = jnp.where(slot - owner_of * CAP == iota((STRIP, SLOTS), 0), 1.0, 0.0).astype(BF16)
    wide = dot(high, spread) * 64.0 + dot(low, spread)
    row = jnp.sum(jnp.where(owner_of[:OWNERS] == iota((OWNERS, SLOTS), 0), wide, 0.0), axis=0, keepdims=True) - 1.0
    wanted_row[...] = row
    store_column(jnp.where(row < 0.0, -2.0, row), picked)
    fill_by_column(pick, picked)

    def ship(which):
        half = which % 2
        for j in range(SELF):
            pltpu.make_async_remote_copy(
                send.at[half, j], recv.at[which, BACK[j]], send_sem.at[which], recv_sem.at[which],
                device_id=(peers[j], col), device_id_type=MESH,
            ).start()
        recv[which, SELF] = send[half, SELF]

    def arrive(which):
        others = recv.at[which, pl.ds(0, OWNERS - 1)]
        pltpu.make_async_copy(others, others, recv_sem.at[which]).wait()
        pltpu.make_async_copy(others, others, send_sem.at[which]).wait()

    def tile(i):
        return pl.ds(pl.multiple_of(i * TILE, TILE), TILE)

    def put(which, i, value):
        send[which % 2, i * EACH:(i + 1) * EACH] = value.astype(BF16).reshape(EACH, CAP, COLS)

    def received(which):
        return recv[which].reshape(SLOTS, COLS)

    def rows_of(s):
        return pl.ds(pl.multiple_of(s * CORE, CORE), CORE)

    def margin_of(s):
        return pl.ds(pl.multiple_of(s * MARGIN, MARGIN), MARGIN)

    def halves(v):
        upper = v.astype(BF16)
        return upper, (v - upper.astype(F32)).astype(BF16)

    def joined(both):
        return both[:, :COLS] + both[:, COLS:]

    def pick_pairs():
        def split(s, _):
            pair[rows_of(s), :COLS], pair[rows_of(s), COLS:] = halves(base[rows_of(s), :])
            return 0

        lax.fori_loop(0, SUBS, split, 0)

        def body(i, _):
            picked[tile(i), :] = joined(dot(pick[tile(i), :], pair[...]))
            return 0

        lax.fori_loop(0, TILES, body, 0)

    def correct_picked(to, which, sign):
        arrived = received(which)
        for i in range(TILES):
            put(to, i, picked[i * TILE:(i + 1) * TILE, :] + sign * dot(same[i * TILE:(i + 1) * TILE, :], arrived))
        ship(to)

    for i in range(TILES):
        put(GATHER, i, dot(pick[i * TILE:(i + 1) * TILE, :], pair[:, :COLS]))
    ship(GATHER)

    @pl.when(jnp.logical_not(stays))
    def _():
        for k in range(2):
            pltpu.make_async_copy(tile_t, tile_t, tile_sem.at[k]).wait()

    for d in range(1, ACROSS):
        pltpu.make_async_remote_copy(
            block.at[col], block.at[col], coarse_sem.at[0], coarse_sem.at[1],
            device_id=(me, lax.rem(col + d, ACROSS)), device_id_type=MESH,
        ).start()

    fill_equal(same, picked, wanted_row)
    fetch_stiff.wait()

    give_x = pltpu.make_async_copy(x, out_x, bring.at[6])

    def iteration(it, _):
        fetch_loads = pltpu.make_async_copy(loads, base, bring.at[5])
        fetch_loads.start()

        def from_core(s, _):
            loc[s, :CORE, :] = x[rows_of(s), :].astype(BF16)
            part[s] = dot(k_v[s, :, :CORE], loc[s, :CORE, :])
            return 0

        lax.fori_loop(0, SUBS, from_core, 0)

        @pl.when(it == ITERS)
        def _():
            give_x.start()

        arrive(GATHER)
        arrived = received(GATHER)
        for s in range(SUBS):
            near = slice(s * MARGIN, (s + 1) * MARGIN)
            margin = dot(take[near, :], arrived).astype(BF16)
            loc[s, CORE:, :] = margin
            outer[near, :] = (part[s, CORE:, :] + dot(k_v[s, CORE:, CORE:], margin)).astype(BF16)
        for i in range(TILES):
            put(SCATTER, i, dot(take_t[i * TILE:(i + 1) * TILE, :], outer[...]))
        ship(SCATTER)
        fetch_loads.wait()

        def core_part(s, _):
            base[rows_of(s), :] = base[rows_of(s), :] - (part[s, :CORE, :] + dot(k_v[s, :CORE, CORE:], loc[s, CORE:, :]))
            return 0

        lax.fori_loop(0, SUBS, core_part, 0)

        @pl.when(it < ITERS)
        def _():
            pick_pairs()

        arrive(SCATTER)

        @pl.when(it < ITERS)
        def _():
            correct_picked(REGATHER, SCATTER, -1.0)

        @pl.when(it == 0)
        def _():
            fill_by_row(pick_t, wanted_row)

        def finish_residual(s, _):
            base[rows_of(s), :] = base[rows_of(s), :] - dot(pick_t[rows_of(s), :], received(SCATTER))

            @pl.when(it == ITERS)
            def _():
                pltpu.make_async_copy(base.at[rows_of(s)], out_r.at[rows_of(s)], bring.at[7]).start()

            return 0

        lax.fori_loop(0, SUBS, finish_residual, 0)

        @pl.when(it < ITERS)
        def _():
            @pl.when(it == 0)
            def _():
                fetch_local.wait()
                for k in range(2):
                    pltpu.make_async_copy(block.at[:3], block.at[:3], coarse_sem.at[k]).wait()

            def solve_core(s, _):
                loc[s, :CORE, :] = base[rows_of(s), :].astype(BF16)
                part[s] = dot(l_v[s, :, :CORE], loc[s, :CORE, :])
                return 0

            lax.fori_loop(0, SUBS, solve_core, 0)
            def finish_margin():
                def solve(s, _):
                    margin = dot(take[margin_of(s), :], received(REGATHER)).astype(BF16)
                    loc[s, CORE:, :] = margin
                    whole = part[s, CORE:, :] + dot(l_v[s, CORE:, CORE:], margin)
                    pair[margin_of(s), :COLS], pair[margin_of(s), COLS:] = halves(0.5 * whole)
                    return 0

                def in_slots(i, _):
                    picked[tile(i), :] = joined(dot(take_t[tile(i), :], pair[:OUTER, :]))
                    return 0

                lax.fori_loop(0, SUBS, solve, 0)
                lax.fori_loop(0, TILES, in_slots, 0)

            def finish_core():
                def solve(s, _):
                    whole = part[s, :CORE, :] + dot(l_v[s, :CORE, CORE:], loc[s, CORE:, :])
                    base[rows_of(s), :] = x[rows_of(s), :] + 0.5 * whole
                    return 0

                lax.fori_loop(0, SUBS, solve, 0)

            projected = jnp.concatenate([dot(mt_v[s, :, :CORE], loc[s, :CORE, :]) for s in range(SUBS)], axis=0)
            arrive(REGATHER)
            proj[pl.ds(at_y, 1)] = (projected + dot(slot_modes_t[...], received(REGATHER))).astype(BF16)[None]
            for dy in (2, 1, 3):
                pltpu.make_async_remote_copy(
                    proj.at[at_y], proj.at[at_y], proj_sem.at[0], proj_sem.at[1],
                    device_id=(lax.rem(at_y + dy, ROWS_Y) * PLANE + at_q, col), device_id_type=MESH,
                ).start()
            finish_margin()
            for k in range(2):
                pltpu.make_async_copy(proj.at[:3], proj.at[:3], proj_sem.at[k]).wait()
            total = dot(block[0], proj[0])
            for k in range(1, ROWS_Y):
                total = total + dot(block[k], proj[k])
            bits[...] = total.astype(BF16).reshape(PLANE, COARSE, COLS)
            for dz, dx in ((1, 2), (0, 2), (1, 1), (1, 3), (1, 0), (0, 1), (0, 3)):
                there = lax.rem(at_z + dz, 2) * 4 + lax.rem(at_x + dx, 4)
                pltpu.make_async_remote_copy(
                    bits.at[there], sums.at[at_q], sum_sem.at[0], sum_sem.at[1],
                    device_id=(at_y * PLANE + there, col), device_id_type=MESH,
                ).start()
            sums[pl.ds(at_q, 1)] = bits[pl.ds(at_q, 1)]
            finish_core()
            for k in range(2):
                pltpu.make_async_copy(sums.at[:PLANE - 1], sums.at[:PLANE - 1], sum_sem.at[k]).wait()
            coarse = sums[0].astype(F32)
            for k in range(1, PLANE):
                coarse = coarse + sums[k].astype(F32)
            coarse = jnp.concatenate(halves(coarse), axis=1)
            for i in range(TILES):
                lifted = joined(dot(slot_modes[i * TILE:(i + 1) * TILE, :], coarse))
                put(CORRECT, i, picked[i * TILE:(i + 1) * TILE, :] + lifted)
            ship(CORRECT)
            for s in range(SUBS):
                lifted = lax.dot_general(
                    mt_v[s, :, :CORE], coarse[s * MODES:(s + 1) * MODES], (((0,), (0,)), ((), ())),
                    preferred_element_type=F32,
                )
                base[s * CORE:(s + 1) * CORE, :] = base[s * CORE:(s + 1) * CORE, :] + joined(lifted)
            pick_pairs()
            arrive(CORRECT)
            correct_picked(GATHER, CORRECT, 1.0)

            def finish_step(s, _):
                x[rows_of(s), :] = base[rows_of(s), :] + dot(pick_t[rows_of(s), :], received(CORRECT))
                return 0

            lax.fori_loop(0, SUBS, finish_step, 0)

        return 0

    lax.fori_loop(0, ITERS + 1, iteration, 0)
    give_x.wait()
    pltpu.make_async_copy(base, out_r, bring.at[7]).wait()


def shards(loads, start, stiffness, local_inverse, modes, coarse_inverse, margin_rows):
    field = jax.ShapeDtypeStruct((HELD, COLS), F32)
    hbm = pl.BlockSpec(memory_space=pl.ANY)
    return pl.pallas_call(
        kernel,
        out_shape=(field, field),
        in_specs=[hbm] * 6 + [pl.BlockSpec(memory_space=pltpu.VMEM)],
        out_specs=(hbm, hbm),
        scratch_shapes=[
            pltpu.VMEM((SUBS, ORDER, ORDER), BF16),
            pltpu.VMEM((SUBS, ORDER, ORDER), BF16),
            pltpu.VMEM((SUBS, MODES, ORDER), BF16),
            pltpu.VMEM((WIDTH, COARSE), BF16),
            pltpu.VMEM((ROWS_Y, WIDTH, COARSE), BF16),
            pltpu.VMEM((HELD, COLS), F32),
            pltpu.VMEM((HELD, COLS), F32),
            pltpu.VMEM((HELD, 2 * COLS), BF16),
            pltpu.VMEM((SUBS, ORDER, COLS), BF16),
            pltpu.VMEM((SUBS, ORDER, COLS), F32),
            pltpu.VMEM((SLOTS, COLS), F32),
            pltpu.VMEM((SLOTS, HELD), BF16),
            pltpu.VMEM((HELD, SLOTS), BF16),
            pltpu.VMEM((SLOTS, SLOTS), BF16),
            pltpu.VMEM((OUTER, SLOTS), BF16),
            pltpu.VMEM((SLOTS, OUTER), BF16),
            pltpu.VMEM((SLOTS, COARSE), BF16),
            pltpu.VMEM((COARSE, SLOTS), BF16),
            pltpu.VMEM((1, OUTER), F32),
            pltpu.VMEM((1, SLOTS), F32),
            pltpu.VMEM((OUTER, COLS), BF16),
            pltpu.VMEM((OWNERS, 8, STRIP), F32),
            pltpu.VMEM((OWNERS, 8, STRIP), F32),
            pltpu.VMEM((2, OWNERS, CAP, COLS), BF16),
            pltpu.VMEM((4, OWNERS, CAP, COLS), BF16),
            pltpu.VMEM((ROWS_Y, COARSE, COLS), BF16),
            pltpu.VMEM((PLANE, COARSE, COLS), BF16),
            pltpu.VMEM((PLANE, COARSE, COLS), BF16),
            pltpu.SemaphoreType.DMA((8,)),
            pltpu.SemaphoreType.DMA((4,)),
            pltpu.SemaphoreType.DMA((4,)),
            pltpu.SemaphoreType.DMA((2,)),
            pltpu.SemaphoreType.DMA((2,)),
            pltpu.SemaphoreType.DMA((2,)),
            pltpu.SemaphoreType.DMA((2,)),
            pltpu.SemaphoreType.DMA((2,)),
        ],
        compiler_params=pltpu.CompilerParams(
            collective_id=0, has_side_effects=True, vmem_limit_bytes=63 * 1024 * 1024
        ),
    )(loads, start, stiffness, local_inverse, jnp.swapaxes(modes, 1, 2), coarse_inverse, margin_rows)


def solution(mesh):
    placed = (
        P("wide", "narrow"),
        P("wide", "narrow"),
        P("wide", None, None),
        P("wide", None, None),
        P("wide", None, None),
        P("wide", "narrow"),
        P("wide", None),
    )
    return jax.shard_map(
        shards,
        mesh=mesh,
        in_specs=placed,
        out_specs=(P("wide", "narrow"), P("wide", "narrow")),
        check_vma=False,
    )
```
